128 devices in a mesh: row: 8 (over z_hi, x), blk: 16 (over z_lo, y, core).
Axes of the slice: x: 4, y: 4, z: 4 (z_hi: 2, z_lo: 2; z = z_hi * 2 + z_lo), core: 2. Of those that a mesh axis runs over, the one named last changes fastest.
Arguments:
- spike_counts: int32 [16384, 2048], P(('row', 'blk')), may hold values from 0 to 23, as said below
- kernel_taps: int32 [16], replicated, may hold values from 1 to 8
- lag_bins: int32 [2], replicated, may hold values from 1 to 32, as said below
Outputs:
- correlogram: bfloat16 [2, 16384, 8, 2048], P(None, 'row', None, 'blk')
The draws below stay inside these ranges and needn't reach their ends.
Inputs may be any that keep to these rules, and one draw needn't show every extreme that they name: `spike_counts`: neurons fire at different rates and share a common drive. `lag_bins`: the second lag equals 32; the first lies between 1 and 31.
All inputs are finite; a program needn't handle non-finite values.
Results may differ from the reference program's by a relative error of at most 0.0034.
Values may be sent and summed in bfloat16 or wider, within the bound.
A program may use at most 128 MiB of HBM per device.

```python
import jax
import jax.numpy as jnp
from jax import lax

NEURONS = 16384
BINS = 2048
TAPS = 16
LAGMAX = 32
PANEL = 2048
N_ROW = 8


def draw_spike_counts(key, part):
    key_rate = jax.random.fold_in(key, 11)
    key_noise = jax.random.fold_in(key, 12)
    key_drive = jax.random.fold_in(key, 13)
    key_share = jax.random.fold_in(key, 14)
    key_where = jax.random.fold_in(key, 15)
    position = jnp.arange(NEURONS, dtype=jnp.int32)[:, None]
    ceiling = 2 + jax.random.randint(key_rate, (NEURONS, 1), 0, 10) + 8 * position // NEURONS
    private = jax.random.randint(key_noise, (NEURONS, BINS), 0, ceiling)
    drive = jax.random.randint(key_drive, (1, BINS), 0, 4)
    share = jax.random.randint(key_share, (NEURONS, 1), 0, 3)
    counts = private + share * drive
    peak_row = jax.random.randint(jax.random.fold_in(key_where, 1), (), 0, NEURONS)
    peak_bin = jax.random.randint(jax.random.fold_in(key_where, 2), (), 0, BINS)
    bin_index = jnp.arange(BINS, dtype=jnp.int32)[None, :]
    counts = jnp.where((position == peak_row) & (bin_index == peak_bin), 23, counts)
    return counts.astype(jnp.int32)


def draw_lag_bins(key, part):
    first = jax.random.randint(jax.random.fold_in(key, 21), (1,), 1, LAGMAX)
    return jnp.concatenate([first, jnp.full((1,), LAGMAX, jnp.int32)]).astype(jnp.int32)


def touch_ends(entries, key, smallest, top_value):
    place = [jax.random.randint(jax.random.fold_in(key, axis), (), 0, length) for axis, length in enumerate(entries.shape)]
    widest = entries.shape.index(max(entries.shape))
    next_to = place[:widest] + [(place[widest] + 1) % entries.shape[widest]] + place[widest + 1:]
    return entries.at[tuple(place)].set(smallest).at[tuple(next_to)].set(top_value)


def setup_inputs(seed: int = 0) -> dict:
    key_of = jax.random.split(jax.random.key(seed), 4)
    return {
        "spike_counts": draw_spike_counts(jax.random.fold_in(key_of[3], 71), 0),
        "kernel_taps": touch_ends(jax.random.randint(key_of[1], (TAPS,), 1, 9), jax.random.fold_in(key_of[1], 1), 1, 8).astype(jnp.int32),
        "lag_bins": draw_lag_bins(jax.random.fold_in(key_of[3], 71), 0),
    }


def smoothed(spike_counts, kernel_taps):
    counts = spike_counts.astype(jnp.float32)
    weights = kernel_taps.astype(jnp.float32) / jnp.sum(kernel_taps.astype(jnp.float32))
    padded = jnp.pad(counts, ((0, 0), (TAPS - 1, 0)))
    result = jnp.zeros_like(counts)
    for delay in range(TAPS):
        result = result + weights[delay] * padded[:, TAPS - 1 - delay:TAPS - 1 - delay + BINS]
    return result

def reference(spike_counts, kernel_taps, lag_bins):
    smooth = smoothed(spike_counts, kernel_taps)
    centred = smooth - lax.optimization_barrier(jnp.mean(smooth, axis=1, keepdims=True))
    population = lax.optimization_barrier(jnp.mean(centred, axis=0))
    residual_part = centred - population[None, :]
    zscored = (residual_part * lax.rsqrt(lax.optimization_barrier(jnp.mean(residual_part * residual_part, axis=1, keepdims=True)) + 1e-05)).astype(jnp.bfloat16)
    zero_pad = jnp.pad(zscored, ((0, 0), (0, BINS)))
    panels = zscored.reshape(N_ROW, PANEL, BINS)
    results = []
    for which in range(2):
        shifted = lax.dynamic_slice_in_dim(zero_pad, lag_bins[which].astype(jnp.int32), BINS, 1)

        def one_panel(rows):
            return (jnp.dot(rows, shifted.T, preferred_element_type=jnp.float32) / BINS).astype(jnp.bfloat16)
        results.append(lax.map(one_panel, panels).reshape(NEURONS, NEURONS))
    return jnp.stack(results).reshape(2, NEURONS, N_ROW, PANEL)
```

```python
import functools

import jax
import jax.numpy as jnp
from jax import lax
from jax.experimental import pallas as pl
from jax.experimental.pallas import tpu as pltpu
from jax.sharding import PartitionSpec as P

NEURONS = 16384
BINS = 2048
TAPS = 16
LAGMAX = 32
MESH = pl.DeviceIdType.MESH
f32 = jnp.float32
bf16 = jnp.bfloat16

ROWS = 128
HALF = ROWS // 2
PAD = 128
CH = 256
NCH = BINS // CH
WIN = CH + PAD

O, XM, XP, X2, PZ, YM, YP, Y2, QZ = range(9)
S_O, S_Z, S_M, S_P, S_2, S_Z2, S_ZM, S_ZP = range(8)


def gather_kernel(taps_ref, lag_ref, counts_ref, acc_ref,
                  raw, bbuf, wz, ws, ft, fr, popt, popr, wrow, wcol, own_sum, part_sum, got1, got2,
                  snd1, rcv1, snd2, rcv2, ssem, rsem):
    row = lax.axis_index("row")
    blk = lax.axis_index("blk")
    zh, x = row // 4, row % 4
    zl, y, c = blk // 8, (blk // 2) % 4, blk % 2

    def at(zh_, x_, zl_, y_, c_):
        return {"row": zh_ * 4 + x_, "blk": zl_ * 8 + y_ * 2 + c_}

    xp = at(zh, (x + 1) % 4, zl, y, c)
    xm = at(zh, (x + 3) % 4, zl, y, c)
    yp = at(zh, x, zl, (y + 1) % 4, c)
    ym = at(zh, x, zl, (y + 3) % 4, c)
    zq = at(zh, x, 1 - zl, y, c)
    zo = at(1 - zh, x, 1 - zl, y, c)
    cp = at(zh, x, zl, y, 1 - c)

    barrier = pltpu.get_barrier_semaphore()
    for d in range(1, 8):
        pl.semaphore_signal(barrier, inc=1, device_id={"row": (row + d) % 8, "blk": blk}, device_id_type=MESH)
    for d in range(1, 16):
        pl.semaphore_signal(barrier, inc=1, device_id={"row": row, "blk": (blk + d) % 16}, device_id_type=MESH)
    pl.semaphore_signal(barrier, inc=1, device_id=zo, device_id_type=MESH)

    def cast(n, _):
        lanes = pl.ds(pl.multiple_of(n * CH, CH), CH)
        part = counts_ref[:, lanes].astype(f32)
        raw[O, :, lanes] = part.astype(bf16)
        own_sum[:, lanes] = jnp.sum(part, axis=0, keepdims=True)
        return 0

    lax.fori_loop(0, NCH, cast, 0)
    pl.semaphore_wait(barrier, 23)

    step1 = [pltpu.make_async_remote_copy(
        src_ref=own_sum, dst_ref=got1.at[d - 1], send_sem=snd1.at[d - 1], recv_sem=rcv1.at[d - 1],
        device_id={"row": (row + d) % 8, "blk": blk}, device_id_type=MESH) for d in range(1, 8)]
    step2 = [pltpu.make_async_remote_copy(
        src_ref=part_sum, dst_ref=got2.at[d - 1], send_sem=snd2.at[d - 1], recv_sem=rcv2.at[d - 1],
        device_id={"row": row, "blk": (blk + d) % 16}, device_id_type=MESH) for d in range(1, 16)]

    copies = {}

    def copy(name, src, dst, device):
        k = len(copies)
        copies[name] = pltpu.make_async_remote_copy(
            src_ref=src, dst_ref=dst, send_sem=ssem.at[k], recv_sem=rsem.at[k],
            device_id=device, device_id_type=MESH)

    def start(*names):
        for name in names:
            copies[name].start()

    def arrived(*names):
        for name in names:
            copies[name].wait_recv()

    def raw_half(slot, h):
        return raw.at[slot, h * HALF:(h + 1) * HALF, :]

    def wz_half(slot, h):
        return wz.at[slot, h * (BINS // 2):(h + 1) * (BINS // 2), :]

    def bb_half(slot, h):
        return bbuf.at[slot * 256 + h * HALF:slot * 256 + (h + 1) * HALF, :]

    def bb_core(slot, h):
        return bbuf.at[slot * 256 + ROWS + h * HALF:slot * 256 + ROWS + (h + 1) * HALF, :]

    def bb_full(slot, other):
        return bbuf.at[slot * 256 + other * ROWS:slot * 256 + (other + 1) * ROWS, :]

    for h in range(2):
        copy(("xp", h), raw_half(O, h), raw_half(XM, h), xp)
        copy(("xm", h), raw_half(O, h), raw_half(XP, h), xm)
        copy(("yp", h), raw_half(O, h), raw_half(YM, h), yp)
        copy(("ym", h), raw_half(O, h), raw_half(YP, h), ym)
        copy(("zq", h), raw_half(O, h), raw_half(QZ, h), zq)
        copy(("zo", h), raw_half(QZ, h), raw_half(PZ, h), zo)
        copy(("pxp", h), wz_half(S_Z, h), wz_half(S_ZM, h), xp)
        copy(("pxm", h), wz_half(S_Z, h), wz_half(S_ZP, h), xm)
        copy(("qyp", h), bb_half(S_Z, h), bb_half(S_ZM, h), yp)
        copy(("qym", h), bb_half(S_Z, h), bb_half(S_ZP, h), ym)
        copy(("cz2", h), bb_half(S_Z2, h), bb_core(S_Z2, h), cp)
    copy("x2p", raw_half(XM, 0), raw_half(X2, 0), xp)
    copy("x2m", raw_half(XP, 1), raw_half(X2, 1), xm)
    copy("y2p", raw_half(YM, 0), raw_half(Y2, 0), yp)
    copy("y2m", raw_half(YP, 1), raw_half(Y2, 1), ym)
    copy("px2p", wz_half(S_ZM, 0), wz_half(S_Z2, 0), xp)
    copy("px2m", wz_half(S_ZP, 1), wz_half(S_Z2, 1), xm)
    copy("qy2p", bb_half(S_ZM, 0), bb_half(S_Z2, 0), yp)
    copy("qy2m", bb_half(S_ZP, 1), bb_half(S_Z2, 1), ym)
    for slot in (S_O, S_Z, S_M, S_P, S_2, S_ZM, S_ZP):
        copy(("c", slot), bb_full(slot, 0), bb_full(slot, 1), cp)

    for s in step1:
        s.start()
    start(("xp", 0), ("xm", 1), ("yp", 0), ("ym", 1), ("zq", 0))

    total = lax.fori_loop(0, TAPS, lambda k, s: s + taps_ref[k], jnp.int32(0)).astype(f32)
    unit = 1.0 / jnp.full((1, 128), total, f32)
    late = lax.broadcasted_iota(jnp.int32, (WIN, CH), 1) + PAD - lax.broadcasted_iota(jnp.int32, (WIN, CH), 0)
    band = jnp.zeros((WIN, CH), f32)
    for k in range(TAPS):
        band = jnp.where(late == k, taps_ref[k].astype(f32), band)
    wrow[...] = band.astype(bf16)
    late = lax.broadcasted_iota(jnp.int32, (CH, WIN), 0) + PAD - lax.broadcasted_iota(jnp.int32, (CH, WIN), 1)
    band = jnp.zeros((CH, WIN), f32)
    for k in range(TAPS):
        band = jnp.where(late == k, taps_ref[k].astype(f32), band)
    wcol[...] = band.astype(bf16)
    ft[BINS:BINS + LAGMAX, :] = jnp.zeros((LAGMAX, 128), f32)
    for k in range(8):
        wz[k, BINS:BINS + LAGMAX, :] = jnp.zeros((LAGMAX, 128), bf16)

    for s in step1:
        s.wait_recv()
    part_sum[...] = own_sum[...] + sum(got1[d] for d in range(7))
    for s in step2:
        s.start()
    start(("xp", 1), ("xm", 0), ("yp", 1), ("ym", 0), ("zq", 1))

    arrived(("xp", 0), ("xm", 1))
    start("x2p", "x2m")
    arrived(("yp", 0), ("ym", 1))
    start("y2p", "y2m")
    arrived(("zq", 0))
    start(("zo", 0))

    for s in step2:
        s.wait_recv()
    alls = part_sum[...] + sum(got2[d] for d in range(15))
    high = alls.astype(bf16)
    rest = alls - high.astype(f32)
    mid = rest.astype(bf16)
    low = (rest - mid.astype(f32)).astype(bf16)
    psum_r = jnp.zeros((8, CH), f32)
    psum_t = jnp.zeros((8, 128), f32)
    edge = jnp.zeros((1, PAD), bf16)
    for n in range(NCH):
        smooth_r = jnp.zeros((16, CH), f32)
        smooth_t = jnp.zeros((CH, 128), f32)
        for piece in (high, mid, low):
            if n == 0:
                win = jnp.concatenate([edge, piece[:, 0:CH]], axis=1)
            else:
                win = piece[:, n * CH - PAD:(n + 1) * CH]
            smooth_r += jnp.dot(jnp.broadcast_to(win, (16, WIN)), wrow[...], preferred_element_type=f32)
            smooth_t += lax.dot_general(wcol[...], jnp.broadcast_to(win, (128, WIN)), (((1,), (1,)), ((), ())),
                                        preferred_element_type=f32)
        popr[:, n * CH:(n + 1) * CH] = smooth_r[0:8]
        popt[n * CH:(n + 1) * CH, :] = smooth_t
        psum_r += smooth_r[0:8]
        psum_t += jnp.sum(smooth_t.reshape(CH // 8, 8, 128), axis=0)
    mean_r = jnp.sum(psum_r, axis=1, keepdims=True) * (1.0 / BINS)
    mean_t = jnp.sum(psum_t, axis=0, keepdims=True) * (1.0 / BINS)
    share = unit * (1.0 / NEURONS)
    popr[...] = (popr[...] - mean_r) * share[:, 0:1]

    def pop_column(n, _):
        rows = pl.ds(pl.multiple_of(n * CH, CH), CH)
        popt[rows, :] = (popt[rows, :] - mean_t) * share
        return 0

    lax.fori_loop(0, NCH, pop_column, 0)

    def to_rows(src, slot):
        dst = slice(slot * 256, slot * 256 + ROWS)

        got = jnp.dot(raw[src, :, 0:CH], wrow[PAD:WIN, :], preferred_element_type=f32)
        fr[:, 0:CH] = got

        def smooth(n, s):
            win = raw[src, :, pl.ds(pl.multiple_of(n * CH - PAD, PAD), WIN)]
            got = jnp.dot(win, wrow[...], preferred_element_type=f32)
            fr[:, pl.ds(pl.multiple_of(n * CH, CH), CH)] = got
            return s + got[:, 0:128] + got[:, 128:256]

        s = lax.fori_loop(1, NCH, smooth, got[:, 0:128] + got[:, 128:256])
        mean = jnp.sum(s, axis=1, keepdims=True) * (1.0 / BINS)

        def centre(n, q):
            lanes = pl.ds(pl.multiple_of(n * CH, CH), CH)
            r = (fr[:, lanes] - mean) * unit[:, 0:1] - popr[0:1, lanes]
            fr[:, lanes] = r
            r = r * r
            return q + r[:, 0:128] + r[:, 128:256]

        q = lax.fori_loop(0, NCH, centre, jnp.zeros((ROWS, 128), f32))
        scale = lax.rsqrt(jnp.sum(q, axis=1, keepdims=True) * (1.0 / BINS) + 1e-05)

        def put(n, _):
            lanes = pl.ds(pl.multiple_of(n * CH, CH), CH)
            bbuf[dst, lanes] = (fr[:, lanes] * scale).astype(bf16)
            return 0

        lax.fori_loop(0, NCH, put, 0)

    lag = lag_ref[0]

    def to_columns(src, slot):
        got = lax.dot_general(wcol[:, PAD:WIN], raw[src, :, 0:CH], (((1,), (1,)), ((), ())),
                              preferred_element_type=f32)
        ft[0:CH, :] = got

        def smooth(n, s):
            win = raw[src, :, pl.ds(pl.multiple_of(n * CH - PAD, PAD), WIN)]
            got = lax.dot_general(wcol[...], win, (((1,), (1,)), ((), ())), preferred_element_type=f32)
            ft[pl.ds(pl.multiple_of(n * CH, CH), CH), :] = got
            return s + jnp.sum(got.reshape(CH // 8, 8, 128), axis=0)

        s = lax.fori_loop(1, NCH, smooth, jnp.sum(got.reshape(CH // 8, 8, 128), axis=0))
        mean = jnp.sum(s, axis=0, keepdims=True) * (1.0 / BINS)

        def centre(n, q):
            rows = pl.ds(pl.multiple_of(n * CH, CH), CH)
            r = (ft[rows, :] - mean) * unit - popt[rows, :]
            ft[rows, :] = r
            return q + jnp.sum((r * r).reshape(CH // 8, 8, 128), axis=0)

        q = lax.fori_loop(0, NCH, centre, jnp.zeros((8, 128), f32))
        scale = lax.rsqrt(jnp.sum(q, axis=0, keepdims=True) * (1.0 / BINS) + 1e-05) * (1.0 / BINS)

        def put(n, _):
            first = pl.multiple_of(n * CH, CH)
            wz[slot, pl.ds(first, CH), :] = (ft[pl.ds(first, CH), :] * scale).astype(bf16)
            ws[slot, pl.ds(first, CH), :] = (ft[pl.ds(first + lag, CH), :] * scale).astype(bf16)
            return 0

        lax.fori_loop(0, NCH, put, 0)

    def move(slot):
        def widen(n, _):
            rows = pl.ds(pl.multiple_of(n * CH, CH), CH)
            ft[rows, :] = wz[slot, rows, :].astype(f32)
            return 0

        def put(n, _):
            first = pl.multiple_of(n * CH, CH)
            ws[slot, pl.ds(first, CH), :] = ft[pl.ds(first + lag, CH), :].astype(bf16)
            return 0

        lax.fori_loop(0, NCH, widen, 0)
        lax.fori_loop(0, NCH, put, 0)

    def place(s, major, minor):
        j, i = s // 2, s % 2
        z = (major + i * ((j + 1) % 2) + j // 3) % 2
        return z * 4 + (minor + (j % 2) * (3 + 2 * i) + (j // 2) * (1 - j % 2) * 2) % 4

    def product(s, pairs, g):
        rows = pairs * 256
        left = bbuf[s * 256:s * 256 + rows, :]
        right = jnp.concatenate([ws[g], wz[g, LAGMAX:LAGMAX + BINS, :]], axis=1)
        out = jnp.dot(left, right, preferred_element_type=f32)
        gg = place(g, zh, x)
        for k in range(2 * pairs):
            here = place(s + k // 2, zl, y) * 2 + (c if k % 2 == 0 else 1 - c)
            there = pl.ds(pl.multiple_of(here * ROWS, ROWS), ROWS)
            part = out[k * ROWS:(k + 1) * ROWS]
            acc_ref[0, gg, there, :] = part[:, 0:128].astype(bf16)
            acc_ref[1, gg, there, :] = part[:, 128:256].astype(bf16)

    def products(s, pairs, first, count):
        def one(g, _):
            product(s, pairs, g)
            return 0
        lax.fori_loop(first, first + count, one, 0)

    to_rows(O, S_O)
    start(("c", S_O))
    to_columns(O, S_O)

    arrived(("zq", 1))
    start(("zo", 1))
    to_rows(QZ, S_Z)
    start(("qyp", 0), ("qyp", 1), ("qym", 1), ("qym", 0), ("c", S_Z))
    arrived(("xp", 1), ("xm", 0), ("yp", 1), ("ym", 0))
    arrived(("zo", 0), ("zo", 1))
    to_columns(PZ, S_Z)
    start(("pxp", 0), ("pxp", 1), ("pxm", 1), ("pxm", 0))
    to_rows(YM, S_M)
    start(("c", S_M))
    to_rows(YP, S_P)
    start(("c", S_P))
    to_columns(XM, S_M)
    to_columns(XP, S_P)
    arrived(("c", S_O), ("c", S_Z))
    products(S_O, 2, 0, 4)
    arrived(("c", S_M), ("c", S_P))
    products(S_M, 2, 0, 4)
    arrived("x2p", "x2m", "y2p", "y2m")
    to_rows(Y2, S_2)
    start(("c", S_2))
    to_columns(X2, S_2)
    arrived(("c", S_2))
    products(S_2, 1, 0, 5)
    products(S_O, 2, S_2, 1)
    products(S_M, 2, S_2, 1)
    arrived(("qyp", 0), ("qym", 1), ("pxp", 0), ("pxm", 1))
    start("qy2p", "qy2m", "px2p", "px2m")
    arrived(("qyp", 1), ("qym", 0), ("pxp", 1), ("pxm", 0))
    start(("c", S_ZM), ("c", S_ZP))
    move(S_ZM)
    move(S_ZP)
    products(S_O, 2, S_ZM, 2)
    products(S_M, 2, S_ZM, 2)
    products(S_2, 1, S_ZM, 2)
    arrived(("c", S_ZM), ("c", S_ZP))
    products(S_ZM, 2, 0, 5)
    products(S_ZM, 2, S_ZM, 2)
    arrived("qy2p", "qy2m")
    start(("cz2", 0), ("cz2", 1))
    arrived("px2p", "px2m")
    move(S_Z2)
    products(S_O, 2, S_Z2, 1)
    products(S_M, 2, S_Z2, 1)
    products(S_ZM, 2, S_Z2, 1)
    products(S_2, 1, S_Z2, 1)
    arrived(("cz2", 0), ("cz2", 1))
    products(S_Z2, 1, 0, 8)

    for s in step1 + step2:
        s.wait_send()
    for name in copies:
        copies[name].wait_send()


N_COPIES = 2 * 11 + 8 + 7


def gathered(taps, lags, counts):
    smem = pl.BlockSpec(memory_space=pltpu.SMEM)
    vmem = pl.BlockSpec(memory_space=pltpu.VMEM)
    dma = pltpu.SemaphoreType.DMA
    return pl.pallas_call(
        gather_kernel,
        out_shape=jax.ShapeDtypeStruct((2, 8, 2048, 128), bf16),
        in_specs=[smem, smem, vmem],
        out_specs=vmem,
        scratch_shapes=[
            pltpu.VMEM((9, ROWS, BINS), bf16),
            pltpu.VMEM((2048, BINS), bf16),
            pltpu.VMEM((8, BINS + LAGMAX, 128), bf16),
            pltpu.VMEM((8, BINS, 128), bf16),
            pltpu.VMEM((BINS + LAGMAX, 128), f32),
            pltpu.VMEM((ROWS, BINS), f32),
            pltpu.VMEM((BINS, 128), f32),
            pltpu.VMEM((8, BINS), f32),
            pltpu.VMEM((WIN, CH), bf16),
            pltpu.VMEM((CH, WIN), bf16),
            pltpu.VMEM((1, BINS), f32),
            pltpu.VMEM((1, BINS), f32),
            pltpu.VMEM((7, 1, BINS), f32),
            pltpu.VMEM((15, 1, BINS), f32),
            dma((7,)), dma((7,)), dma((15,)), dma((15,)),
            dma((N_COPIES,)), dma((N_COPIES,)),
        ],
        compiler_params=pltpu.CompilerParams(
            collective_id=0, has_side_effects=True, vmem_limit_bytes=44 << 20),
        name="gather_products",
    )(taps, lags, counts)


def layout_kernel(acc_ref, out_ref):
    out_ref[0] = jnp.swapaxes(acc_ref[0].astype(f32), 0, 1).astype(bf16)


def laid_out(acc):
    rows = 512
    return pl.pallas_call(
        layout_kernel,
        out_shape=jax.ShapeDtypeStruct((2, 2048, 8, 128), bf16),
        grid=(2, 2048 // rows),
        in_specs=[pl.BlockSpec((1, 8, rows, 128), lambda l, i: (l, 0, i, 0))],
        out_specs=pl.BlockSpec((1, rows, 8, 128), lambda l, i: (l, i, 0, 0)),
        compiler_params=pltpu.CompilerParams(vmem_limit_bytes=16 << 20),
        name="layout",
    )(acc)


def shards(spike_counts, kernel_taps, lag_bins):
    return laid_out(gathered(kernel_taps, lag_bins, spike_counts))


def solution(mesh):
    placed = (P(("row", "blk"), None), P(), P())
    return jax.shard_map(
        shards, mesh=mesh, in_specs=placed, out_specs=P(None, "row", None, "blk"), check_vma=False
    )
```

```python
import functools

import jax
import jax.numpy as jnp
from jax import lax
from jax.experimental import pallas as pl
from jax.experimental.pallas import tpu as pltpu
from jax.sharding import PartitionSpec as P

NEURONS = 16384
BINS = 2048
TAPS = 16
LAGMAX = 32
MESH = pl.DeviceIdType.MESH
f32 = jnp.float32
bf16 = jnp.bfloat16

ROWS = 128
HALF = ROWS // 2
PAD = 128
CH = 256
NCH = BINS // CH
WIN = CH + PAD
QUARTER = ROWS // 4

O, XM, XP, X2, PZ, YM, YP, Y2, QZ = range(9)
S_O, S_Z, S_M, S_P, S_2, S_Z2, S_ZM, S_ZP = range(8)


def gather_kernel(taps_hbm, lag_hbm, counts_hbm, acc_ref,
                  taps_ref, lag_ref, counts, raw, bbuf, wz, ws, ft, fr, popt, popr, wrow, wcol, wsum,
                  own_sum, part_sum, got1, got2, lsem, snd1, rcv1, snd2, rcv2, ssem, rsem):
    row = lax.axis_index("row")
    blk = lax.axis_index("blk")
    zh, x = row // 4, row % 4
    zl, y, c = blk // 8, (blk // 2) % 4, blk % 2

    loads = [pltpu.make_async_copy(counts_hbm.at[h * HALF:(h + 1) * HALF, :],
                                   counts.at[h * HALF:(h + 1) * HALF, :], lsem.at[h]) for h in range(2)]
    loads += [pltpu.make_async_copy(taps_hbm, taps_ref, lsem.at[2]),
              pltpu.make_async_copy(lag_hbm, lag_ref, lsem.at[3])]
    for load in loads:
        load.start()

    def at(zh_, x_, zl_, y_, c_):
        return {"row": zh_ * 4 + x_, "blk": zl_ * 8 + y_ * 2 + c_}

    xp = at(zh, (x + 1) % 4, zl, y, c)
    xm = at(zh, (x + 3) % 4, zl, y, c)
    yp = at(zh, x, zl, (y + 1) % 4, c)
    ym = at(zh, x, zl, (y + 3) % 4, c)
    zq = at(zh, x, 1 - zl, y, c)
    zo = at(1 - zh, x, 1 - zl, y, c)
    cp = at(zh, x, zl, y, 1 - c)

    barrier = pltpu.get_barrier_semaphore()
    for d in range(1, 8):
        pl.semaphore_signal(barrier, inc=1, device_id={"row": (row + d) % 8, "blk": blk}, device_id_type=MESH)
    for d in range(1, 16):
        pl.semaphore_signal(barrier, inc=1, device_id={"row": row, "blk": (blk + d) % 16}, device_id_type=MESH)
    pl.semaphore_signal(barrier, inc=1, device_id=zo, device_id_type=MESH)

    for h in range(2):
        loads[h].wait()
        for n in range(NCH):
            part = counts[h * HALF:(h + 1) * HALF, n * CH:(n + 1) * CH].astype(f32)
            raw[O, h * HALF:(h + 1) * HALF, n * CH:(n + 1) * CH] = part.astype(bf16)
            part = jnp.sum(part, axis=0, keepdims=True)
            own_sum[:, n * CH:(n + 1) * CH] = part if h == 0 else own_sum[:, n * CH:(n + 1) * CH] + part
    pl.semaphore_wait(barrier, 23)

    step1 = [pltpu.make_async_remote_copy(
        src_ref=own_sum, dst_ref=got1.at[d - 1], send_sem=snd1.at[d - 1], recv_sem=rcv1.at[d - 1],
        device_id={"row": (row + d) % 8, "blk": blk}, device_id_type=MESH) for d in range(1, 8)]
    step2 = [pltpu.make_async_remote_copy(
        src_ref=part_sum, dst_ref=got2.at[d - 1], send_sem=snd2.at[d - 1], recv_sem=rcv2.at[d - 1],
        device_id={"row": row, "blk": (blk + d) % 16}, device_id_type=MESH) for d in range(1, 16)]

    copies = {}

    def copy(name, src, dst, device):
        k = len(copies)
        copies[name] = pltpu.make_async_remote_copy(
            src_ref=src, dst_ref=dst, send_sem=ssem.at[k], recv_sem=rsem.at[k],
            device_id=device, device_id_type=MESH)

    def start(*names):
        for name in names:
            copies[name].start()

    def arrived(*names):
        for name in names:
            copies[name].wait_recv()

    def raw_half(slot, h):
        return raw.at[slot, h * HALF:(h + 1) * HALF, :]

    def raw_quarter(slot, k):
        return raw.at[slot, k * QUARTER:(k + 1) * QUARTER, :]

    def wz_half(slot, h):
        return wz.at[slot, h * (BINS // 2):(h + 1) * (BINS // 2), :]

    def bb_half(slot, h, other=0):
        first = slot * 256 + other * ROWS + h * HALF
        return bbuf.at[first:first + HALF, :]

    for h in range(2):
        copy(("xp", h), raw_half(O, h), raw_half(XM, h), xp)
        copy(("xm", h), raw_half(O, h), raw_half(XP, h), xm)
        copy(("yp", h), raw_half(O, h), raw_half(YM, h), yp)
        copy(("ym", h), raw_half(O, h), raw_half(YP, h), ym)
        copy(("pxp", h), wz_half(S_Z, h), wz_half(S_ZM, h), xp)
        copy(("pxm", h), wz_half(S_Z, h), wz_half(S_ZP, h), xm)
        copy(("qyp", h), bb_half(S_Z, h), bb_half(S_ZM, h), yp)
        copy(("qym", h), bb_half(S_Z, h), bb_half(S_ZP, h), ym)
        copy(("zy", h), bb_half(S_2, h), bb_half(S_Z2, h), zq)
        for slot in (S_Z2, S_ZM, S_ZP):
            copy(("c", slot, h), bb_half(slot, h), bb_half(slot, h, 1), cp)
    for k in range(4):
        copy(("zq", k), raw_quarter(O, k), raw_quarter(QZ, k), zq)
        copy(("zo", k), raw_quarter(QZ, k), raw_quarter(PZ, k), zo)
    copy("x2p", raw_half(XM, 0), raw_half(X2, 0), xp)
    copy("x2m", raw_half(XP, 1), raw_half(X2, 1), xm)
    copy("y2p", raw_half(YM, 0), raw_half(Y2, 0), yp)
    copy("y2m", raw_half(YP, 1), raw_half(Y2, 1), ym)
    copy("px2p", wz_half(S_ZM, 0), wz_half(S_Z2, 0), xp)
    copy("px2m", wz_half(S_ZP, 1), wz_half(S_Z2, 1), xm)
    for slot in (S_O, S_Z, S_M, S_P, S_2):
        copy(("c", slot), bbuf.at[slot * 256:slot * 256 + ROWS, :],
             bbuf.at[slot * 256 + ROWS:slot * 256 + 2 * ROWS, :], cp)

    for s in step1:
        s.start()
    start(("zq", 0), ("xp", 0), ("xm", 1), ("yp", 0), ("ym", 1), ("zq", 1))

    loads[2].wait()
    loads[3].wait()
    taps = [taps_ref[k].astype(f32) for k in range(TAPS)]
    total = sum(taps[1:], taps[0])
    unit = 1.0 / jnp.full((8, 128), total, f32)
    late = lax.broadcasted_iota(jnp.int32, (WIN, CH), 1) + PAD - lax.broadcasted_iota(jnp.int32, (WIN, CH), 0)
    band = jnp.zeros((WIN, CH), f32)
    for k in range(TAPS):
        band = jnp.where(late == k, taps[k], band)
    wrow[...] = band.astype(bf16)
    late = lax.broadcasted_iota(jnp.int32, (CH, WIN), 0) + PAD - lax.broadcasted_iota(jnp.int32, (CH, WIN), 1)
    band = jnp.zeros((CH, WIN), f32)
    for k in range(TAPS):
        band = jnp.where(late == k, taps[k], band)
    wcol[...] = band.astype(bf16)
    wsum[...] = jnp.full((BINS, 128), total, f32).astype(bf16)
    left = TAPS - lax.broadcasted_iota(jnp.int32, (TAPS, 128), 0)
    edge = jnp.zeros((TAPS, 128), f32)
    for k in range(TAPS):
        edge = edge + jnp.where(left > k, taps[k], 0.0)
    wsum[BINS - TAPS:BINS, :] = edge.astype(bf16)
    ft[BINS:BINS + LAGMAX, :] = jnp.zeros((LAGMAX, 128), f32)
    for k in range(8):
        wz[k, BINS:BINS + LAGMAX, :] = jnp.zeros((LAGMAX, 128), bf16)

    for s in step1:
        s.wait_recv()
    part_sum[...] = own_sum[...] + sum([got1[d] for d in range(1, 7)], got1[0])
    for s in step2:
        s.start()
    start(("zq", 2), ("xp", 1), ("xm", 0), ("yp", 1), ("ym", 0), ("zq", 3))
    arrived(("zq", 0))
    start(("zo", 0))
    arrived(("xp", 0), ("xm", 1))
    start("x2p", "x2m")
    arrived(("yp", 0), ("ym", 1))
    start("y2p", "y2m")
    arrived(("zq", 1))
    start(("zo", 1))

    for s in step2:
        s.wait_recv()
    alls = part_sum[...] + sum([got2[d] for d in range(1, 15)], got2[0])
    high = alls.astype(bf16)
    rest = alls - high.astype(f32)
    mid = rest.astype(bf16)
    low = (rest - mid.astype(f32)).astype(bf16)
    summed = jnp.zeros((8, 128), f32)
    for n in range(NCH):
        first = max(n * CH - PAD, 0)
        wins = jnp.concatenate(
            [jnp.broadcast_to(piece[:, first:(n + 1) * CH], (16, (n + 1) * CH - first)) for piece in (high, mid, low)],
            axis=0)
        got = jnp.dot(wins, wrow[PAD:WIN, :] if n == 0 else wrow[...], preferred_element_type=f32)
        got = (got[0:8] + got[16:24]) + got[32:40]
        popr[:, n * CH:(n + 1) * CH] = got
        summed = summed + (got[:, 0:128] + got[:, 128:256])
    mean_pop = jnp.sum(summed, axis=1, keepdims=True) * (1.0 / BINS)
    popr[...] = (popr[...] - mean_pop) * (1.0 / NEURONS)
    for n in range(BINS // 128):
        popt[n * 128:(n + 1) * 128, :] = jnp.transpose(
            jnp.broadcast_to(popr[0:1, n * 128:(n + 1) * 128], (128, 128)))

    def to_rows(src, slot):
        mean = jnp.dot(raw[src], wsum[...], preferred_element_type=f32) * (1.0 / BINS)
        mean = jnp.concatenate([mean, mean], axis=1)
        q = jnp.zeros((ROWS, 128), f32)
        for n in range(NCH):
            if n == 0:
                got = jnp.dot(raw[src, :, 0:CH], wrow[PAD:WIN, :], preferred_element_type=f32)
            else:
                got = jnp.dot(raw[src, :, n * CH - PAD:(n + 1) * CH], wrow[...], preferred_element_type=f32)
            r = got - mean - popr[0:1, n * CH:(n + 1) * CH]
            fr[:, n * CH:(n + 1) * CH] = r
            r = r * r
            q = q + r[:, 0:128] + r[:, 128:256]
        u = unit[0:1, 0:1]
        scale = lax.rsqrt(jnp.sum(q, axis=1, keepdims=True) * (1.0 / BINS) * (u * u) + 1e-05) * u
        for n in range(NCH):
            bbuf[slot * 256:slot * 256 + ROWS, n * CH:(n + 1) * CH] = (
                fr[:, n * CH:(n + 1) * CH] * scale).astype(bf16)

    lag = lag_ref[0]

    def to_columns(src, slot):
        mean = jnp.transpose(jnp.dot(raw[src], wsum[...], preferred_element_type=f32) * (1.0 / BINS))[0:8]
        q = jnp.zeros((4, 8, 128), f32)
        for n in range(NCH):
            if n == 0:
                got = lax.dot_general(wcol[:, PAD:WIN], raw[src, :, 0:CH], (((1,), (1,)), ((), ())),
                                      preferred_element_type=f32)
            else:
                got = lax.dot_general(wcol[...], raw[src, :, n * CH - PAD:(n + 1) * CH], (((1,), (1,)), ((), ())),
                                      preferred_element_type=f32)
            r = got.reshape(32, 8, 128) - mean[None] - popt[n * CH:(n + 1) * CH, :].reshape(32, 8, 128)
            ft[n * CH:(n + 1) * CH, :] = r.reshape(CH, 128)
            r = r * r
            for j in range(8):
                q = q + r[4 * j:4 * j + 4]
        q = (q[0] + q[1]) + (q[2] + q[3])
        u = unit[0:1]
        scale = lax.rsqrt(jnp.sum(q, axis=0, keepdims=True) * (1.0 / BINS) * (u * u) + 1e-05) * u * (1.0 / BINS)
        for n in range(NCH):
            wz[slot, n * CH:(n + 1) * CH, :] = (ft[n * CH:(n + 1) * CH, :] * scale).astype(bf16)
            ws[slot, n * CH:(n + 1) * CH, :] = (ft[pl.ds(n * CH + lag, CH), :] * scale).astype(bf16)

    def move(slot):
        for n in range(NCH):
            ft[n * CH:(n + 1) * CH, :] = wz[slot, n * CH:(n + 1) * CH, :].astype(f32)
        for n in range(NCH):
            ws[slot, n * CH:(n + 1) * CH, :] = ft[pl.ds(n * CH + lag, CH), :].astype(bf16)

    def place(s, major, minor):
        j, i = s // 2, s % 2
        z = (major + i * ((j + 1) % 2) + j // 3) % 2
        return z * 4 + (minor + (j % 2) * (3 + 2 * i) + (j // 2) * (1 - j % 2) * 2) % 4

    def whole(s, pairs=1):
        return [(s * 256 + k * ROWS, ROWS, (place(s + k // 2, zl, y) * 2 + (c if k % 2 == 0 else 1 - c)) * ROWS)
                for k in range(2 * pairs)]

    def halves(s, h):
        return [(s * 256 + k * ROWS + h * HALF, HALF, (place(s, zl, y) * 2 + (c if k == 0 else 1 - c)) * ROWS + h * HALF)
                for k in range(2)]

    def multiply(segments, groups):
        runs = []
        for first, size, _ in segments:
            if runs and isinstance(first, int) and runs[-1][0] + runs[-1][1] == first:
                runs[-1][1] += size
            else:
                runs.append([first, size])
        left = [bbuf[first:first + size, :] if isinstance(first, int) else bbuf[pl.ds(first, size), :]
                for first, size in runs]
        left = left[0] if len(left) == 1 else jnp.concatenate(left, axis=0)
        for g in groups:
            right = jnp.concatenate([ws[g], wz[g, LAGMAX:LAGMAX + BINS, :]], axis=1)
            out = jnp.dot(left, right, preferred_element_type=f32)
            gg, k = place(g, zh, x), 0
            for _, size, there in segments:
                there = pl.ds(pl.multiple_of(there, size), size)
                acc_ref[0, gg, there, :] = out[k:k + size, 0:128].astype(bf16)
                acc_ref[1, gg, there, :] = out[k:k + size, 128:256].astype(bf16)
                k += size

    def multiply_pairs(first, count, pairs, groups):
        def one(n, _):
            s = first + n * pairs
            start_row = pl.multiple_of(s * 256, 256)
            left = bbuf[pl.ds(start_row, pairs * 256), :]
            for g in groups:
                right = jnp.concatenate([ws[g], wz[g, LAGMAX:LAGMAX + BINS, :]], axis=1)
                out = jnp.dot(left, right, preferred_element_type=f32)
                gg = place(g, zh, x)
                for k, (_, size, there) in enumerate(whole(s, pairs)):
                    there = pl.ds(pl.multiple_of(there, size), size)
                    acc_ref[0, gg, there, :] = out[k * size:(k + 1) * size, 0:128].astype(bf16)
                    acc_ref[1, gg, there, :] = out[k * size:(k + 1) * size, 128:256].astype(bf16)
            return 0
        lax.fori_loop(0, count, one, 0)

    to_rows(O, S_O)
    start(("c", S_O))
    arrived(("zq", 2))
    start(("zo", 2))
    to_columns(O, S_O)
    arrived(("zq", 3))
    start(("zo", 3))
    to_rows(QZ, S_Z)
    start(("qyp", 0), ("qym", 1), ("qyp", 1), ("qym", 0), ("c", S_Z))
    arrived(("xp", 1), ("xm", 0), ("yp", 1), ("ym", 0))
    to_rows(YM, S_M)
    start(("c", S_M))
    to_rows(YP, S_P)
    start(("c", S_P))
    to_columns(XM, S_M)
    to_columns(XP, S_P)
    arrived(("zo", 0), ("zo", 1), ("zo", 2), ("zo", 3))
    to_columns(PZ, S_Z)
    start(("pxp", 0), ("pxm", 1), ("pxp", 1), ("pxm", 0))
    arrived(("c", S_O), ("c", S_Z))
    multiply_pairs(S_O, 2, 1, (S_O, S_Z, S_M, S_P))
    arrived("y2p", "y2m")
    to_rows(Y2, S_2)
    start(("zy", 0), ("zy", 1), ("c", S_2))
    arrived("x2p", "x2m")
    to_columns(X2, S_2)
    arrived(("c", S_M), ("c", S_P), ("c", S_2))
    multiply_pairs(S_M, 3, 1, (S_O, S_Z, S_M, S_P))
    multiply(whole(S_O, 5), (S_2,))
    arrived(("qyp", 0), ("qym", 1))
    start(("c", S_ZM, 0), ("c", S_ZP, 1))
    arrived(("pxp", 0), ("pxm", 1))
    start("px2p", "px2m")
    arrived(("c", S_ZM, 0), ("c", S_ZP, 1))
    multiply(halves(S_ZM, 0) + halves(S_ZP, 1), (S_O, S_Z, S_M, S_P, S_2))
    arrived(("qyp", 1), ("qym", 0))
    start(("c", S_ZM, 1), ("c", S_ZP, 0))
    arrived(("pxp", 1), ("pxm", 0))
    move(S_ZM)
    move(S_ZP)
    multiply_pairs(S_O, 2, 2, (S_ZM, S_ZP))
    arrived(("zy", 0), ("zy", 1))
    start(("c", S_Z2, 0), ("c", S_Z2, 1))
    arrived(("c", S_ZM, 1), ("c", S_ZP, 0))
    multiply(halves(S_ZM, 1) + halves(S_ZP, 0), (S_O, S_Z, S_M, S_P, S_2))
    multiply(whole(S_2) + whole(S_ZM, 2), (S_ZM, S_ZP))
    arrived(("c", S_Z2, 0), ("c", S_Z2, 1))
    multiply(whole(S_Z2), (S_O, S_Z, S_M, S_P, S_2, S_ZM, S_ZP))
    arrived("px2p", "px2m")
    move(S_Z2)
    multiply_pairs(S_O, 2, 4, (S_Z2,))

    for s in step1 + step2:
        s.wait_send()
    for name in copies:
        copies[name].wait_send()


N_COPIES = 2 * 12 + 8 + 6 + 5


def gathered(taps, lags, counts):
    dma = pltpu.SemaphoreType.DMA
    return pl.pallas_call(
        gather_kernel,
        out_shape=jax.ShapeDtypeStruct((2, 8, 2048, 128), bf16),
        in_specs=[pl.BlockSpec(memory_space=pltpu.HBM)] * 3,
        out_specs=pl.BlockSpec(memory_space=pltpu.VMEM),
        scratch_shapes=[
            pltpu.SMEM((TAPS,), jnp.int32),
            pltpu.SMEM((2,), jnp.int32),
            pltpu.VMEM((ROWS, BINS), jnp.int32),
            pltpu.VMEM((9, ROWS, BINS), bf16),
            pltpu.VMEM((2048, BINS), bf16),
            pltpu.VMEM((8, BINS + LAGMAX, 128), bf16),
            pltpu.VMEM((8, BINS, 128), bf16),
            pltpu.VMEM((BINS + LAGMAX, 128), f32),
            pltpu.VMEM((ROWS, BINS), f32),
            pltpu.VMEM((BINS, 128), f32),
            pltpu.VMEM((8, BINS), f32),
            pltpu.VMEM((WIN, CH), bf16),
            pltpu.VMEM((CH, WIN), bf16),
            pltpu.VMEM((BINS, 128), bf16),
            pltpu.VMEM((1, BINS), f32),
            pltpu.VMEM((1, BINS), f32),
            pltpu.VMEM((7, 1, BINS), f32),
            pltpu.VMEM((15, 1, BINS), f32),
            dma((4,)), dma((7,)), dma((7,)), dma((15,)), dma((15,)),
            dma((N_COPIES,)), dma((N_COPIES,)),
        ],
        compiler_params=pltpu.CompilerParams(
            collective_id=0, has_side_effects=True, vmem_limit_bytes=44 << 20),
        name="gather_products",
    )(*(pltpu.with_memory_space_constraint(a, pltpu.HBM) for a in (taps, lags, counts)))


def layout_kernel(acc_ref, out_ref, buf, sem):
    rows, slots = buf.shape[1], buf.shape[0]
    steps = 2048 // rows
    puts = []
    for s in range(2 * steps):
        lag, first = s // steps, (s % steps) * rows
        if s >= slots:
            puts[s - slots].wait()
        buf[s % slots] = jnp.swapaxes(acc_ref[lag, :, first:first + rows, :].astype(f32), 0, 1).astype(bf16)
        put = pltpu.make_async_copy(buf.at[s % slots], out_ref.at[lag, first:first + rows], sem.at[s % slots])
        put.start()
        puts.append(put)
    for put in puts[-slots:]:
        put.wait()


def laid_out(acc):
    rows, slots = 256, 4
    return pl.pallas_call(
        layout_kernel,
        out_shape=jax.ShapeDtypeStruct((2, 2048, 8, 128), bf16),
        in_specs=[pl.BlockSpec(memory_space=pltpu.VMEM)],
        out_specs=pl.BlockSpec(memory_space=pl.ANY),
        scratch_shapes=[pltpu.VMEM((slots, rows, 8, 128), bf16), pltpu.SemaphoreType.DMA((slots,))],
        compiler_params=pltpu.CompilerParams(vmem_limit_bytes=24 << 20),
        name="layout",
    )(acc)


def shards(spike_counts, kernel_taps, lag_bins):
    return laid_out(gathered(kernel_taps, lag_bins, spike_counts))


def solution(mesh):
    placed = (P(("row", "blk"), None), P(), P())
    return jax.shard_map(
        shards, mesh=mesh, in_specs=placed, out_specs=P(None, "row", None, "blk"), check_vma=False
    )
```

```python
import functools

import jax
import jax.numpy as jnp
from jax import lax
from jax.experimental import pallas as pl
from jax.experimental.pallas import tpu as pltpu
from jax.sharding import PartitionSpec as P

NEURONS = 16384
BINS = 2048
TAPS = 16
LAGMAX = 32
MESH = pl.DeviceIdType.MESH
f32 = jnp.float32
bf16 = jnp.bfloat16

ROWS = 128
HALF = ROWS // 2
PAD = 128
CH = 256
NCH = BINS // CH
WIN = CH + PAD
QUARTER = ROWS // 4

O, XM, XP, X2, PZ, YM, YP, Y2, QZ = range(9)
S_O, S_Z, S_M, S_P, S_2, S_Z2, S_ZM, S_ZP = range(8)


def gather_kernel(taps_hbm, lag_hbm, counts_hbm, acc_ref,
                  taps_ref, lag_ref, counts, raw, bbuf, wz, ws, via, ft, fr, popt, popr, wrow, wcol, wsum,
                  own_sum, part_sum, got1, got2, lsem, snd1, rcv1, snd2, rcv2, ssem, rsem):
    row = lax.axis_index("row")
    blk = lax.axis_index("blk")
    zh, x = row // 4, row % 4
    zl, y, c = blk // 8, (blk // 2) % 4, blk % 2

    loads = [pltpu.make_async_copy(counts_hbm.at[h * HALF:(h + 1) * HALF, :],
                                   counts.at[h * HALF:(h + 1) * HALF, :], lsem.at[h]) for h in range(2)]
    loads += [pltpu.make_async_copy(taps_hbm, taps_ref, lsem.at[2]),
              pltpu.make_async_copy(lag_hbm, lag_ref, lsem.at[3])]
    for load in loads:
        load.start()

    def at(zh_, x_, zl_, y_, c_):
        return {"row": zh_ * 4 + x_, "blk": zl_ * 8 + y_ * 2 + c_}

    xp = at(zh, (x + 1) % 4, zl, y, c)
    xm = at(zh, (x + 3) % 4, zl, y, c)
    yp = at(zh, x, zl, (y + 1) % 4, c)
    ym = at(zh, x, zl, (y + 3) % 4, c)
    zq = at(zh, x, 1 - zl, y, c)
    zo = at(1 - zh, x, 1 - zl, y, c)
    cp = at(zh, x, zl, y, 1 - c)

    barrier = pltpu.get_barrier_semaphore()
    for d in range(1, 8):
        pl.semaphore_signal(barrier, inc=1, device_id={"row": (row + d) % 8, "blk": blk}, device_id_type=MESH)
    for d in range(1, 16):
        pl.semaphore_signal(barrier, inc=1, device_id={"row": row, "blk": (blk + d) % 16}, device_id_type=MESH)
    pl.semaphore_signal(barrier, inc=1, device_id=zo, device_id_type=MESH)

    for h in range(2):
        loads[h].wait()
        for n in range(NCH):
            part = counts[h * HALF:(h + 1) * HALF, n * CH:(n + 1) * CH].astype(f32)
            raw[O, h * HALF:(h + 1) * HALF, n * CH:(n + 1) * CH] = part.astype(bf16)
            part = jnp.sum(part, axis=0, keepdims=True)
            own_sum[:, n * CH:(n + 1) * CH] = part if h == 0 else own_sum[:, n * CH:(n + 1) * CH] + part
    pl.semaphore_wait(barrier, 23)

    step1 = [pltpu.make_async_remote_copy(
        src_ref=own_sum, dst_ref=got1.at[d - 1], send_sem=snd1.at[d - 1], recv_sem=rcv1.at[d - 1],
        device_id={"row": (row + d) % 8, "blk": blk}, device_id_type=MESH) for d in range(1, 8)]
    step2 = [pltpu.make_async_remote_copy(
        src_ref=part_sum, dst_ref=got2.at[d - 1], send_sem=snd2.at[d - 1], recv_sem=rcv2.at[d - 1],
        device_id={"row": row, "blk": (blk + d) % 16}, device_id_type=MESH) for d in range(1, 16)]

    copies = {}

    def copy(name, src, dst, device):
        k = len(copies)
        copies[name] = pltpu.make_async_remote_copy(
            src_ref=src, dst_ref=dst, send_sem=ssem.at[k], recv_sem=rsem.at[k],
            device_id=device, device_id_type=MESH)

    def start(*names):
        for name in names:
            copies[name].start()

    def arrived(*names):
        for name in names:
            copies[name].wait_recv()

    def raw_half(slot, h):
        return raw.at[slot, h * HALF:(h + 1) * HALF, :]

    def raw_quarter(slot, k):
        return raw.at[slot, k * QUARTER:(k + 1) * QUARTER, :]

    def wz_half(slot, h):
        return wz.at[slot, h * (BINS // 2):(h + 1) * (BINS // 2), :]

    def bb_half(slot, h, other=0):
        first = slot * 256 + other * ROWS + h * HALF
        return bbuf.at[first:first + HALF, :]

    def bb_rows(slot, first, size):
        return bbuf.at[slot * 256 + first:slot * 256 + first + size, :]

    for h in range(2):
        copy(("xp", h), raw_half(O, h), raw_half(XM, h), xp)
        copy(("xm", h), raw_half(O, h), raw_half(XP, h), xm)
        copy(("yp", h), raw_half(O, h), raw_half(YM, h), yp)
        copy(("ym", h), raw_half(O, h), raw_half(YP, h), ym)
        copy(("qyp", h), bb_half(S_Z, h), bb_half(S_ZM, h), yp)
        copy(("qym", h), bb_half(S_Z, h), bb_half(S_ZP, h), ym)
        for slot in (S_ZM, S_ZP):
            copy(("c", slot, h), bb_half(slot, h), bb_half(slot, h, 1), cp)
    for k in range(4):
        copy(("zq", k), raw_quarter(O, k), raw_quarter(QZ, k), zq)
        copy(("zo", k), raw_quarter(QZ, k), raw_quarter(PZ, k), zo)
    copy("x2p", raw_half(XM, 0), raw_half(X2, 0), xp)
    copy("x2m", raw_half(XP, 1), raw_half(X2, 1), xm)
    copy("y2p", raw_half(YM, 0), raw_half(Y2, 0), yp)
    copy("y2m", raw_half(YP, 1), raw_half(Y2, 1), ym)
    copy("a1", wz_half(S_M, 0), via.at[0], zq)
    copy("a2", via.at[0], wz_half(S_ZM, 0), zo)
    copy("b1", wz_half(S_P, 1), via.at[1], zo)
    copy("b2", via.at[1], wz_half(S_ZP, 1), zq)
    copy("pxp", wz_half(S_Z, 1), wz_half(S_ZM, 1), xp)
    copy("pxm", wz_half(S_Z, 0), wz_half(S_ZP, 0), xm)
    copy("px2p", wz_half(S_ZM, 1), wz_half(S_Z2, 1), xp)
    copy("px2m", wz_half(S_ZP, 0), wz_half(S_Z2, 0), xm)
    copy("qy2p", bb_rows(S_ZM, 0, QUARTER), bb_rows(S_Z2, 0, QUARTER), yp)
    copy("qy2m", bb_rows(S_ZP, 3 * QUARTER, QUARTER), bb_rows(S_Z2, 3 * QUARTER, QUARTER), ym)
    copy("zy", bb_rows(S_2, QUARTER, HALF), bb_rows(S_Z2, QUARTER, HALF), zq)
    for k, size in ((0, QUARTER), (QUARTER, HALF), (3 * QUARTER, QUARTER)):
        copy(("c", S_Z2, k), bb_rows(S_Z2, k, size), bb_rows(S_Z2, ROWS + k, size), cp)
    for slot in (S_O, S_Z, S_M, S_P, S_2):
        copy(("c", slot), bbuf.at[slot * 256:slot * 256 + ROWS, :],
             bbuf.at[slot * 256 + ROWS:slot * 256 + 2 * ROWS, :], cp)

    for s in step1:
        s.start()
    start(("zq", 0), ("xp", 0), ("xm", 1), ("yp", 0), ("ym", 1), ("zq", 1))

    loads[2].wait()
    loads[3].wait()
    taps = [taps_ref[k].astype(f32) for k in range(TAPS)]
    total = sum(taps[1:], taps[0])
    unit = 1.0 / jnp.full((8, 128), total, f32)
    late = lax.broadcasted_iota(jnp.int32, (WIN, CH), 1) + PAD - lax.broadcasted_iota(jnp.int32, (WIN, CH), 0)
    band = jnp.zeros((WIN, CH), f32)
    for k in range(TAPS):
        band = jnp.where(late == k, taps[k], band)
    wrow[...] = band.astype(bf16)
    late = lax.broadcasted_iota(jnp.int32, (CH, WIN), 0) + PAD - lax.broadcasted_iota(jnp.int32, (CH, WIN), 1)
    band = jnp.zeros((CH, WIN), f32)
    for k in range(TAPS):
        band = jnp.where(late == k, taps[k], band)
    wcol[...] = band.astype(bf16)
    wsum[...] = jnp.full((BINS, 128), total, f32).astype(bf16)
    left = TAPS - lax.broadcasted_iota(jnp.int32, (TAPS, 128), 0)
    edge = jnp.zeros((TAPS, 128), f32)
    for k in range(TAPS):
        edge = edge + jnp.where(left > k, taps[k], 0.0)
    wsum[BINS - TAPS:BINS, :] = edge.astype(bf16)
    ft[BINS:BINS + LAGMAX, :] = jnp.zeros((LAGMAX, 128), f32)
    for k in range(8):
        wz[k, BINS:BINS + LAGMAX, :] = jnp.zeros((LAGMAX, 128), bf16)

    for s in step1:
        s.wait_recv()
    part_sum[...] = own_sum[...] + sum([got1[d] for d in range(1, 7)], got1[0])
    for s in step2:
        s.start()
    start(("zq", 2), ("xp", 1), ("xm", 0), ("yp", 1), ("ym", 0), ("zq", 3))
    arrived(("zq", 0))
    start(("zo", 0))
    arrived(("xp", 0), ("xm", 1))
    start("x2p", "x2m")
    arrived(("yp", 0), ("ym", 1))
    start("y2p", "y2m")
    arrived(("zq", 1))
    start(("zo", 1))

    for s in step2:
        s.wait_recv()
    alls = part_sum[...] + sum([got2[d] for d in range(1, 15)], got2[0])
    high = alls.astype(bf16)
    rest = alls - high.astype(f32)
    mid = rest.astype(bf16)
    low = (rest - mid.astype(f32)).astype(bf16)
    summed = jnp.zeros((8, 128), f32)
    for n in range(NCH):
        first = max(n * CH - PAD, 0)
        wins = jnp.concatenate(
            [jnp.broadcast_to(piece[:, first:(n + 1) * CH], (16, (n + 1) * CH - first)) for piece in (high, mid, low)],
            axis=0)
        got = jnp.dot(wins, wrow[PAD:WIN, :] if n == 0 else wrow[...], preferred_element_type=f32)
        got = (got[0:8] + got[16:24]) + got[32:40]
        popr[:, n * CH:(n + 1) * CH] = got
        summed = summed + (got[:, 0:128] + got[:, 128:256])
    mean_pop = jnp.sum(summed, axis=1, keepdims=True) * (1.0 / BINS)
    popr[...] = (popr[...] - mean_pop) * (1.0 / NEURONS)
    for n in range(BINS // 128):
        popt[n * 128:(n + 1) * 128, :] = jnp.transpose(
            jnp.broadcast_to(popr[0:1, n * 128:(n + 1) * 128], (128, 128)))

    def to_rows(src, slot):
        mean = jnp.dot(raw[src], wsum[...], preferred_element_type=f32) * (1.0 / BINS)
        mean = jnp.concatenate([mean, mean], axis=1)
        q = jnp.zeros((ROWS, 128), f32)
        for n in range(NCH):
            if n == 0:
                got = jnp.dot(raw[src, :, 0:CH], wrow[PAD:WIN, :], preferred_element_type=f32)
            else:
                got = jnp.dot(raw[src, :, n * CH - PAD:(n + 1) * CH], wrow[...], preferred_element_type=f32)
            r = got - mean - popr[0:1, n * CH:(n + 1) * CH]
            fr[:, n * CH:(n + 1) * CH] = r
            r = r * r
            q = q + r[:, 0:128] + r[:, 128:256]
        u = unit[0:1, 0:1]
        scale = lax.rsqrt(jnp.sum(q, axis=1, keepdims=True) * (1.0 / BINS) * (u * u) + 1e-05) * u
        for n in range(NCH):
            bbuf[slot * 256:slot * 256 + ROWS, n * CH:(n + 1) * CH] = (
                fr[:, n * CH:(n + 1) * CH] * scale).astype(bf16)

    lag = lag_ref[0]

    def to_columns(src, slot):
        mean = jnp.transpose(jnp.dot(raw[src], wsum[...], preferred_element_type=f32) * (1.0 / BINS))[0:8]
        q = jnp.zeros((4, 8, 128), f32)
        for n in range(NCH):
            if n == 0:
                got = lax.dot_general(wcol[:, PAD:WIN], raw[src, :, 0:CH], (((1,), (1,)), ((), ())),
                                      preferred_element_type=f32)
            else:
                got = lax.dot_general(wcol[...], raw[src, :, n * CH - PAD:(n + 1) * CH], (((1,), (1,)), ((), ())),
                                      preferred_element_type=f32)
            r = got.reshape(32, 8, 128) - mean[None] - popt[n * CH:(n + 1) * CH, :].reshape(32, 8, 128)
            ft[n * CH:(n + 1) * CH, :] = r.reshape(CH, 128)
            r = r * r
            for j in range(8):
                q = q + r[4 * j:4 * j + 4]
        q = (q[0] + q[1]) + (q[2] + q[3])
        u = unit[0:1]
        scale = lax.rsqrt(jnp.sum(q, axis=0, keepdims=True) * (1.0 / BINS) * (u * u) + 1e-05) * u * (1.0 / BINS)
        for n in range(NCH):
            wz[slot, n * CH:(n + 1) * CH, :] = (ft[n * CH:(n + 1) * CH, :] * scale).astype(bf16)
            ws[slot, n * CH:(n + 1) * CH, :] = (ft[pl.ds(n * CH + lag, CH), :] * scale).astype(bf16)

    def move(slot):
        for n in range(NCH):
            ft[n * CH:(n + 1) * CH, :] = wz[slot, n * CH:(n + 1) * CH, :].astype(f32)
        for n in range(NCH):
            ws[slot, n * CH:(n + 1) * CH, :] = ft[pl.ds(n * CH + lag, CH), :].astype(bf16)

    def place(s, major, minor):
        j, i = s // 2, s % 2
        z = (major + i * ((j + 1) % 2) + j // 3) % 2
        return z * 4 + (minor + (j % 2) * (3 + 2 * i) + (j // 2) * (1 - j % 2) * 2) % 4

    def whole(s, pairs=1):
        return [(s * 256 + k * ROWS, ROWS, (place(s + k // 2, zl, y) * 2 + (c if k % 2 == 0 else 1 - c)) * ROWS)
                for k in range(2 * pairs)]

    def halves(s, h):
        return [(s * 256 + k * ROWS + h * HALF, HALF, (place(s, zl, y) * 2 + (c if k == 0 else 1 - c)) * ROWS + h * HALF)
                for k in range(2)]

    def multiply(segments, groups):
        runs = []
        for first, size, _ in segments:
            if runs and isinstance(first, int) and runs[-1][0] + runs[-1][1] == first:
                runs[-1][1] += size
            else:
                runs.append([first, size])
        left = [bbuf[first:first + size, :] if isinstance(first, int) else bbuf[pl.ds(first, size), :]
                for first, size in runs]
        left = left[0] if len(left) == 1 else jnp.concatenate(left, axis=0)
        for g in groups:
            right = jnp.concatenate([ws[g], wz[g, LAGMAX:LAGMAX + BINS, :]], axis=1)
            out = jnp.dot(left, right, preferred_element_type=f32)
            gg, k = place(g, zh, x), 0
            for _, size, there in segments:
                there = pl.ds(pl.multiple_of(there, size), size)
                acc_ref[0, gg, there, :] = out[k:k + size, 0:128].astype(bf16)
                acc_ref[1, gg, there, :] = out[k:k + size, 128:256].astype(bf16)
                k += size

    def multiply_pairs(first, count, pairs, groups):
        def one(n, _):
            s = first + n * pairs
            start_row = pl.multiple_of(s * 256, 256)
            left = bbuf[pl.ds(start_row, pairs * 256), :]
            for g in groups:
                right = jnp.concatenate([ws[g], wz[g, LAGMAX:LAGMAX + BINS, :]], axis=1)
                out = jnp.dot(left, right, preferred_element_type=f32)
                gg = place(g, zh, x)
                for k, (_, size, there) in enumerate(whole(s, pairs)):
                    there = pl.ds(pl.multiple_of(there, size), size)
                    acc_ref[0, gg, there, :] = out[k * size:(k + 1) * size, 0:128].astype(bf16)
                    acc_ref[1, gg, there, :] = out[k * size:(k + 1) * size, 128:256].astype(bf16)
            return 0
        lax.fori_loop(0, count, one, 0)

    near = (S_O, S_Z, S_M, S_P)
    to_rows(O, S_O)
    start(("c", S_O))
    arrived(("zq", 2))
    start(("zo", 2))
    to_columns(O, S_O)
    arrived(("zq", 3))
    start(("zo", 3))
    to_rows(QZ, S_Z)
    start(("qyp", 0), ("qym", 1), ("qyp", 1), ("qym", 0), ("c", S_Z))
    arrived(("xp", 1), ("xm", 0))
    to_columns(XM, S_M)
    start("a1")
    to_columns(XP, S_P)
    start("b1")
    arrived(("yp", 1), ("ym", 0))
    to_rows(YM, S_M)
    start(("c", S_M))
    arrived(("zo", 0), ("zo", 1), ("zo", 2), ("zo", 3))
    to_columns(PZ, S_Z)
    start("pxp", "pxm")
    to_rows(YP, S_P)
    start(("c", S_P))
    arrived(("c", S_O), ("c", S_Z))
    multiply_pairs(S_O, 2, 1, near)
    arrived("y2p", "y2m")
    to_rows(Y2, S_2)
    start(("c", S_2))
    arrived("a1", "b1")
    start("a2", "b2", "zy")
    arrived("x2p", "x2m")
    to_columns(X2, S_2)
    arrived(("c", S_M), ("c", S_P))
    multiply_pairs(S_M, 2, 1, near)
    arrived(("qyp", 0), ("qym", 1))
    start("qy2p", "qy2m", ("c", S_ZM, 0), ("c", S_ZP, 1))
    arrived("pxp", "pxm")
    start("px2p", "px2m")
    arrived(("c", S_2))
    multiply(whole(S_2), near)
    multiply(whole(S_O, 5), (S_2,))
    arrived(("c", S_ZM, 0), ("c", S_ZP, 1))
    early = halves(S_ZM, 0) + halves(S_ZP, 1)
    later = halves(S_ZM, 1) + halves(S_ZP, 0)
    multiply(early, near + (S_2,))
    arrived("a2")
    move(S_ZM)
    multiply(whole(S_O, 5) + early, (S_ZM,))
    arrived(("qyp", 1), ("qym", 0))
    start(("c", S_ZM, 1), ("c", S_ZP, 0))
    arrived("px2p", "px2m")
    move(S_Z2)
    multiply(whole(S_O, 5) + early, (S_Z2,))
    arrived("qy2p", "qy2m")
    start(("c", S_Z2, 0), ("c", S_Z2, 3 * QUARTER))
    arrived(("c", S_ZM, 1), ("c", S_ZP, 0))
    multiply(later, near + (S_2, S_ZM, S_Z2))
    arrived("b2")
    move(S_ZP)
    arrived("zy")
    start(("c", S_Z2, QUARTER))
    multiply(whole(S_O, 5) + whole(S_ZM, 2), (S_ZP,))
    arrived(("c", S_Z2, 0), ("c", S_Z2, QUARTER), ("c", S_Z2, 3 * QUARTER))
    multiply(whole(S_Z2), near + (S_2, S_ZM, S_Z2, S_ZP))

    for s in step1 + step2:
        s.wait_send()
    for name in copies:
        copies[name].wait_send()


N_COPIES = 2 * 8 + 8 + 4 + 8 + 3 + 3 + 5


def gathered(taps, lags, counts):
    dma = pltpu.SemaphoreType.DMA
    return pl.pallas_call(
        gather_kernel,
        out_shape=jax.ShapeDtypeStruct((2, 8, 2048, 128), bf16),
        in_specs=[pl.BlockSpec(memory_space=pltpu.HBM)] * 3,
        out_specs=pl.BlockSpec(memory_space=pltpu.VMEM),
        scratch_shapes=[
            pltpu.SMEM((TAPS,), jnp.int32),
            pltpu.SMEM((2,), jnp.int32),
            pltpu.VMEM((ROWS, BINS), jnp.int32),
            pltpu.VMEM((9, ROWS, BINS), bf16),
            pltpu.VMEM((2048, BINS), bf16),
            pltpu.VMEM((8, BINS + LAGMAX, 128), bf16),
            pltpu.VMEM((8, BINS, 128), bf16),
            pltpu.VMEM((2, BINS // 2, 128), bf16),
            pltpu.VMEM((BINS + LAGMAX, 128), f32),
            pltpu.VMEM((ROWS, BINS), f32),
            pltpu.VMEM((BINS, 128), f32),
            pltpu.VMEM((8, BINS), f32),
            pltpu.VMEM((WIN, CH), bf16),
            pltpu.VMEM((CH, WIN), bf16),
            pltpu.VMEM((BINS, 128), bf16),
            pltpu.VMEM((1, BINS), f32),
            pltpu.VMEM((1, BINS), f32),
            pltpu.VMEM((7, 1, BINS), f32),
            pltpu.VMEM((15, 1, BINS), f32),
            dma((4,)), dma((7,)), dma((7,)), dma((15,)), dma((15,)),
            dma((N_COPIES,)), dma((N_COPIES,)),
        ],
        compiler_params=pltpu.CompilerParams(
            collective_id=0, has_side_effects=True, vmem_limit_bytes=44 << 20),
        name="gather_products",
    )(*(pltpu.with_memory_space_constraint(a, pltpu.HBM) for a in (taps, lags, counts)))


def layout_kernel(acc_ref, out_ref, buf, sem):
    rows, slots = buf.shape[1], buf.shape[0]
    steps = 2048 // rows
    puts = []
    for s in range(2 * steps):
        lag, first = s // steps, (s % steps) * rows
        if s >= slots:
            puts[s - slots].wait()
        buf[s % slots] = jnp.swapaxes(acc_ref[lag, :, first:first + rows, :].astype(f32), 0, 1).astype(bf16)
        put = pltpu.make_async_copy(buf.at[s % slots], out_ref.at[lag, first:first + rows], sem.at[s % slots])
        put.start()
        puts.append(put)
    for put in puts[-slots:]:
        put.wait()


def laid_out(acc):
    rows, slots = 256, 4
    return pl.pallas_call(
        layout_kernel,
        out_shape=jax.ShapeDtypeStruct((2, 2048, 8, 128), bf16),
        in_specs=[pl.BlockSpec(memory_space=pltpu.VMEM)],
        out_specs=pl.BlockSpec(memory_space=pl.ANY),
        scratch_shapes=[pltpu.VMEM((slots, rows, 8, 128), bf16), pltpu.SemaphoreType.DMA((slots,))],
        compiler_params=pltpu.CompilerParams(vmem_limit_bytes=24 << 20),
        name="layout",
    )(acc)


def shards(spike_counts, kernel_taps, lag_bins):
    return laid_out(gathered(kernel_taps, lag_bins, spike_counts))


def solution(mesh):
    placed = (P(("row", "blk"), None), P(), P())
    return jax.shard_map(
        shards, mesh=mesh, in_specs=placed, out_specs=P(None, "row", None, "blk"), check_vma=False
    )
```

```python
import functools

import jax
import jax.numpy as jnp
from jax import lax
from jax.experimental import pallas as pl
from jax.experimental.pallas import tpu as pltpu
from jax.sharding import PartitionSpec as P

NEURONS = 16384
BINS = 2048
TAPS = 16
LAGMAX = 32
MESH = pl.DeviceIdType.MESH
f32 = jnp.float32
bf16 = jnp.bfloat16

ROWS = 128
HALF = ROWS // 2
PAD = 128
CH = 256
NCH = BINS // CH
WIN = CH + PAD
QUARTER = ROWS // 4

O, XM, XP, X2, PZ, YM, YP, Y2, QZ = range(9)
S_O, S_Z, S_M, S_P, S_2, S_Z2, S_ZM, S_ZP = range(8)


def gather_kernel(taps_hbm, lag_hbm, counts_hbm, acc_ref,
                  taps_ref, lag_ref, counts, raw, bbuf, wz, ws, ft, fr, popt, popr, wrow, wcol, wsum,
                  own_sum, part_sum, got1, got2, lsem, snd1, rcv1, snd2, rcv2, ssem, rsem):
    row = lax.axis_index("row")
    blk = lax.axis_index("blk")
    zh, x = row // 4, row % 4
    zl, y, c = blk // 8, (blk // 2) % 4, blk % 2

    loads = [pltpu.make_async_copy(counts_hbm.at[h * HALF:(h + 1) * HALF, :],
                                   counts.at[h * HALF:(h + 1) * HALF, :], lsem.at[h]) for h in range(2)]
    loads += [pltpu.make_async_copy(taps_hbm, taps_ref, lsem.at[2]),
              pltpu.make_async_copy(lag_hbm, lag_ref, lsem.at[3])]
    for load in loads:
        load.start()

    def at(zh_, x_, zl_, y_, c_):
        return {"row": zh_ * 4 + x_, "blk": zl_ * 8 + y_ * 2 + c_}

    xp = at(zh, (x + 1) % 4, zl, y, c)
    xm = at(zh, (x + 3) % 4, zl, y, c)
    yp = at(zh, x, zl, (y + 1) % 4, c)
    ym = at(zh, x, zl, (y + 3) % 4, c)
    zq = at(zh, x, 1 - zl, y, c)
    zo = at(1 - zh, x, 1 - zl, y, c)
    cp = at(zh, x, zl, y, 1 - c)

    barrier = pltpu.get_barrier_semaphore()
    for d in range(1, 8):
        pl.semaphore_signal(barrier, inc=1, device_id={"row": (row + d) % 8, "blk": blk}, device_id_type=MESH)
    for d in range(1, 16):
        pl.semaphore_signal(barrier, inc=1, device_id={"row": row, "blk": (blk + d) % 16}, device_id_type=MESH)
    pl.semaphore_signal(barrier, inc=1, device_id=zo, device_id_type=MESH)

    for h in range(2):
        loads[h].wait()
        for n in range(NCH):
            part = counts[h * HALF:(h + 1) * HALF, n * CH:(n + 1) * CH].astype(f32)
            raw[O, h * HALF:(h + 1) * HALF, n * CH:(n + 1) * CH] = part.astype(bf16)
            part = jnp.sum(part, axis=0, keepdims=True)
            own_sum[:, n * CH:(n + 1) * CH] = part if h == 0 else own_sum[:, n * CH:(n + 1) * CH] + part
    pl.semaphore_wait(barrier, 23)

    step1 = [pltpu.make_async_remote_copy(
        src_ref=own_sum, dst_ref=got1.at[d - 1], send_sem=snd1.at[d - 1], recv_sem=rcv1.at[d - 1],
        device_id={"row": (row + d) % 8, "blk": blk}, device_id_type=MESH) for d in range(1, 8)]
    step2 = [pltpu.make_async_remote_copy(
        src_ref=part_sum, dst_ref=got2.at[d - 1], send_sem=snd2.at[d - 1], recv_sem=rcv2.at[d - 1],
        device_id={"row": row, "blk": (blk + d) % 16}, device_id_type=MESH) for d in range(1, 16)]

    copies = {}

    def copy(name, src, dst, device):
        k = len(copies)
        copies[name] = pltpu.make_async_remote_copy(
            src_ref=src, dst_ref=dst, send_sem=ssem.at[k], recv_sem=rsem.at[k],
            device_id=device, device_id_type=MESH)

    def start(*names):
        for name in names:
            copies[name].start()

    def arrived(*names):
        for name in names:
            copies[name].wait_recv()

    def raw_half(slot, h):
        return raw.at[slot, h * HALF:(h + 1) * HALF, :]

    def raw_quarter(slot, k):
        return raw.at[slot, k * QUARTER:(k + 1) * QUARTER, :]

    def wz_half(slot, h):
        return wz.at[slot, h * (BINS // 2):(h + 1) * (BINS // 2), :]

    def bb_half(slot, h, other=0):
        first = slot * 256 + other * ROWS + h * HALF
        return bbuf.at[first:first + HALF, :]

    for h in range(2):
        copy(("xp", h), raw_half(O, h), raw_half(XM, h), xp)
        copy(("xm", h), raw_half(O, h), raw_half(XP, h), xm)
        copy(("yp", h), raw_half(O, h), raw_half(YM, h), yp)
        copy(("ym", h), raw_half(O, h), raw_half(YP, h), ym)
        copy(("pxp", h), wz_half(S_Z, h), wz_half(S_ZM, h), xp)
        copy(("pxm", h), wz_half(S_Z, h), wz_half(S_ZP, h), xm)
        copy(("qyp", h), bb_half(S_Z, h), bb_half(S_ZM, h), yp)
        copy(("qym", h), bb_half(S_Z, h), bb_half(S_ZP, h), ym)
        copy(("zy", h), bb_half(S_2, h), bb_half(S_Z2, h), zq)
        for slot in (S_Z2, S_ZM, S_ZP):
            copy(("c", slot, h), bb_half(slot, h), bb_half(slot, h, 1), cp)
    for k in range(4):
        copy(("zq", k), raw_quarter(O, k), raw_quarter(QZ, k), zq)
        copy(("zo", k), raw_quarter(QZ, k), raw_quarter(PZ, k), zo)
    copy("x2p", raw_half(XM, 0), raw_half(X2, 0), xp)
    copy("x2m", raw_half(XP, 1), raw_half(X2, 1), xm)
    copy("y2p", raw_half(YM, 0), raw_half(Y2, 0), yp)
    copy("y2m", raw_half(YP, 1), raw_half(Y2, 1), ym)
    copy("px2p", wz_half(S_ZM, 0), wz_half(S_Z2, 0), xp)
    copy("px2m", wz_half(S_ZP, 1), wz_half(S_Z2, 1), xm)
    for slot in (S_O, S_Z, S_M, S_P, S_2):
        copy(("c", slot), bbuf.at[slot * 256:slot * 256 + ROWS, :],
             bbuf.at[slot * 256 + ROWS:slot * 256 + 2 * ROWS, :], cp)

    for s in step1:
        s.start()
    start(("zq", 0), ("xp", 0), ("xm", 1), ("yp", 0), ("ym", 1), ("zq", 1))

    loads[2].wait()
    loads[3].wait()
    taps = [taps_ref[k].astype(f32) for k in range(TAPS)]
    total = sum(taps[1:], taps[0])
    unit = 1.0 / jnp.full((8, 128), total, f32)
    late = lax.broadcasted_iota(jnp.int32, (WIN, CH), 1) + PAD - lax.broadcasted_iota(jnp.int32, (WIN, CH), 0)
    band = jnp.zeros((WIN, CH), f32)
    for k in range(TAPS):
        band = jnp.where(late == k, taps[k], band)
    wrow[...] = band.astype(bf16)
    late = lax.broadcasted_iota(jnp.int32, (CH, WIN), 0) + PAD - lax.broadcasted_iota(jnp.int32, (CH, WIN), 1)
    band = jnp.zeros((CH, WIN), f32)
    for k in range(TAPS):
        band = jnp.where(late == k, taps[k], band)
    wcol[...] = band.astype(bf16)
    wsum[...] = jnp.full((BINS, 128), total, f32).astype(bf16)
    left = TAPS - lax.broadcasted_iota(jnp.int32, (TAPS, 128), 0)
    edge = jnp.zeros((TAPS, 128), f32)
    for k in range(TAPS):
        edge = edge + jnp.where(left > k, taps[k], 0.0)
    wsum[BINS - TAPS:BINS, :] = edge.astype(bf16)
    ft[BINS:BINS + LAGMAX, :] = jnp.zeros((LAGMAX, 128), f32)
    for k in range(8):
        wz[k, BINS:BINS + LAGMAX, :] = jnp.zeros((LAGMAX, 128), bf16)

    for s in step1:
        s.wait_recv()
    part_sum[...] = own_sum[...] + sum([got1[d] for d in range(1, 7)], got1[0])
    for s in step2:
        s.start()
    start(("zq", 2), ("xp", 1), ("xm", 0), ("yp", 1), ("ym", 0), ("zq", 3))
    arrived(("zq", 0))
    start(("zo", 0))
    arrived(("xp", 0), ("xm", 1))
    start("x2p", "x2m")
    arrived(("yp", 0), ("ym", 1))
    start("y2p", "y2m")
    arrived(("zq", 1))
    start(("zo", 1))
    arrived(("zq", 2))
    start(("zo", 2))

    for s in step2:
        s.wait_recv()
    alls = part_sum[...] + sum([got2[d] for d in range(1, 15)], got2[0])
    high = alls.astype(bf16)
    rest = alls - high.astype(f32)
    mid = rest.astype(bf16)
    low = (rest - mid.astype(f32)).astype(bf16)
    summed = jnp.zeros((8, 128), f32)
    for n in range(NCH):
        first = max(n * CH - PAD, 0)
        wins = jnp.concatenate(
            [jnp.broadcast_to(piece[:, first:(n + 1) * CH], (16, (n + 1) * CH - first)) for piece in (high, mid, low)],
            axis=0)
        got = jnp.dot(wins, wrow[PAD:WIN, :] if n == 0 else wrow[...], preferred_element_type=f32)
        got = (got[0:8] + got[16:24]) + got[32:40]
        popr[:, n * CH:(n + 1) * CH] = got
        summed = summed + (got[:, 0:128] + got[:, 128:256])
    mean_pop = jnp.sum(summed, axis=1, keepdims=True) * (1.0 / BINS)
    popr[...] = (popr[...] - mean_pop) * (1.0 / NEURONS)
    for n in range(BINS // 128):
        popt[n * 128:(n + 1) * 128, :] = jnp.transpose(
            jnp.broadcast_to(popr[0:1, n * 128:(n + 1) * 128], (128, 128)))

    def to_rows(src, slot):
        mean = jnp.dot(raw[src], wsum[...], preferred_element_type=f32) * (1.0 / BINS)
        mean = jnp.concatenate([mean, mean], axis=1)
        q = jnp.zeros((ROWS, 128), f32)
        for n in range(NCH):
            if n == 0:
                got = jnp.dot(raw[src, :, 0:CH], wrow[PAD:WIN, :], preferred_element_type=f32)
            else:
                got = jnp.dot(raw[src, :, n * CH - PAD:(n + 1) * CH], wrow[...], preferred_element_type=f32)
            r = got - mean - popr[0:1, n * CH:(n + 1) * CH]
            fr[:, n * CH:(n + 1) * CH] = r
            r = r * r
            q = q + r[:, 0:128] + r[:, 128:256]
        u = unit[0:1, 0:1]
        scale = lax.rsqrt(jnp.sum(q, axis=1, keepdims=True) * (1.0 / BINS) * (u * u) + 1e-05) * u
        for n in range(NCH):
            bbuf[slot * 256:slot * 256 + ROWS, n * CH:(n + 1) * CH] = (
                fr[:, n * CH:(n + 1) * CH] * scale).astype(bf16)

    lag = lag_ref[0]

    def to_columns(src, slot):
        mean = jnp.transpose(jnp.dot(raw[src], wsum[...], preferred_element_type=f32) * (1.0 / BINS))[0:8]
        q = jnp.zeros((4, 8, 128), f32)
        for n in range(NCH):
            if n == 0:
                got = lax.dot_general(wcol[:, PAD:WIN], raw[src, :, 0:CH], (((1,), (1,)), ((), ())),
                                      preferred_element_type=f32)
            else:
                got = lax.dot_general(wcol[...], raw[src, :, n * CH - PAD:(n + 1) * CH], (((1,), (1,)), ((), ())),
                                      preferred_element_type=f32)
            r = got.reshape(32, 8, 128) - mean[None] - popt[n * CH:(n + 1) * CH, :].reshape(32, 8, 128)
            ft[n * CH:(n + 1) * CH, :] = r.reshape(CH, 128)
            r = r * r
            for j in range(8):
                q = q + r[4 * j:4 * j + 4]
        q = (q[0] + q[1]) + (q[2] + q[3])
        u = unit[0:1]
        scale = lax.rsqrt(jnp.sum(q, axis=0, keepdims=True) * (1.0 / BINS) * (u * u) + 1e-05) * u * (1.0 / BINS)
        for n in range(NCH):
            wz[slot, n * CH:(n + 1) * CH, :] = (ft[n * CH:(n + 1) * CH, :] * scale).astype(bf16)
            ws[slot, n * CH:(n + 1) * CH, :] = (ft[pl.ds(n * CH + lag, CH), :] * scale).astype(bf16)

    def move(slot):
        for n in range(NCH):
            ft[n * CH:(n + 1) * CH, :] = wz[slot, n * CH:(n + 1) * CH, :].astype(f32)
        for n in range(NCH):
            ws[slot, n * CH:(n + 1) * CH, :] = ft[pl.ds(n * CH + lag, CH), :].astype(bf16)

    def place(s, major, minor):
        j, i = s // 2, s % 2
        z = (major + i * ((j + 1) % 2) + j // 3) % 2
        return z * 4 + (minor + (j % 2) * (3 + 2 * i) + (j // 2) * (1 - j % 2) * 2) % 4

    def whole(s, pairs=1):
        return [(s * 256 + k * ROWS, ROWS, (place(s + k // 2, zl, y) * 2 + (c if k % 2 == 0 else 1 - c)) * ROWS)
                for k in range(2 * pairs)]

    def halves(s, h):
        return [(s * 256 + k * ROWS + h * HALF, HALF, (place(s, zl, y) * 2 + (c if k == 0 else 1 - c)) * ROWS + h * HALF)
                for k in range(2)]

    def multiply(segments, groups):
        runs = []
        for first, size, _ in segments:
            if runs and isinstance(first, int) and runs[-1][0] + runs[-1][1] == first:
                runs[-1][1] += size
            else:
                runs.append([first, size])
        left = [bbuf[first:first + size, :] if isinstance(first, int) else bbuf[pl.ds(first, size), :]
                for first, size in runs]
        left = left[0] if len(left) == 1 else jnp.concatenate(left, axis=0)
        for g in groups:
            right = jnp.concatenate([ws[g], wz[g, LAGMAX:LAGMAX + BINS, :]], axis=1)
            out = jnp.dot(left, right, preferred_element_type=f32)
            gg, k = place(g, zh, x), 0
            for _, size, there in segments:
                there = pl.ds(pl.multiple_of(there, size), size)
                acc_ref[0, gg, there, :] = out[k:k + size, 0:128].astype(bf16)
                acc_ref[1, gg, there, :] = out[k:k + size, 128:256].astype(bf16)
                k += size

    def multiply_pairs(first, count, pairs, groups):
        def one(n, _):
            s = first + n * pairs
            start_row = pl.multiple_of(s * 256, 256)
            left = bbuf[pl.ds(start_row, pairs * 256), :]
            for g in groups:
                right = jnp.concatenate([ws[g], wz[g, LAGMAX:LAGMAX + BINS, :]], axis=1)
                out = jnp.dot(left, right, preferred_element_type=f32)
                gg = place(g, zh, x)
                for k, (_, size, there) in enumerate(whole(s, pairs)):
                    there = pl.ds(pl.multiple_of(there, size), size)
                    acc_ref[0, gg, there, :] = out[k * size:(k + 1) * size, 0:128].astype(bf16)
                    acc_ref[1, gg, there, :] = out[k * size:(k + 1) * size, 128:256].astype(bf16)
            return 0
        lax.fori_loop(0, count, one, 0)

    near = (S_O, S_Z, S_M, S_P)
    to_rows(O, S_O)
    start(("c", S_O))
    arrived(("zq", 3))
    start(("zo", 3))
    to_rows(QZ, S_Z)
    start(("qyp", 0), ("qym", 1), ("qyp", 1), ("qym", 0), ("c", S_Z))
    to_columns(O, S_O)
    arrived(("xp", 1), ("xm", 0), ("yp", 1), ("ym", 0))
    to_columns(XM, S_M)
    to_columns(XP, S_P)
    to_rows(YM, S_M)
    start(("c", S_M))
    arrived(("zo", 0), ("zo", 1), ("zo", 2), ("zo", 3))
    to_columns(PZ, S_Z)
    start(("pxp", 0), ("pxm", 1), ("pxp", 1), ("pxm", 0))
    to_rows(YP, S_P)
    start(("c", S_P))
    arrived("y2p", "y2m")
    to_rows(Y2, S_2)
    start(("zy", 0), ("zy", 1), ("c", S_2))
    arrived(("c", S_O), ("c", S_Z))
    multiply_pairs(S_O, 2, 1, near)
    arrived("x2p", "x2m")
    to_columns(X2, S_2)
    arrived(("c", S_M), ("c", S_P), ("c", S_2))
    multiply_pairs(S_M, 3, 1, near)
    arrived(("qyp", 0), ("qym", 1))
    start(("c", S_ZM, 0), ("c", S_ZP, 1))
    arrived(("pxp", 0), ("pxm", 1))
    start("px2p", "px2m")
    multiply(whole(S_O, 5), (S_2,))
    early = halves(S_ZM, 0) + halves(S_ZP, 1)
    later = halves(S_ZM, 1) + halves(S_ZP, 0)
    arrived(("c", S_ZM, 0), ("c", S_ZP, 1))
    multiply(early, near + (S_2,))
    arrived(("qyp", 1), ("qym", 0))
    start(("c", S_ZM, 1), ("c", S_ZP, 0))
    arrived(("pxp", 1), ("pxm", 0))
    move(S_ZM)
    move(S_ZP)
    multiply_pairs(S_O, 2, 2, (S_ZM, S_ZP))
    multiply(whole(S_2) + early, (S_ZM, S_ZP))
    arrived(("zy", 0), ("zy", 1))
    start(("c", S_Z2, 0), ("c", S_Z2, 1))
    arrived(("c", S_ZM, 1), ("c", S_ZP, 0))
    multiply(later, near + (S_2, S_ZM, S_ZP))
    arrived(("c", S_Z2, 0), ("c", S_Z2, 1))
    multiply(whole(S_Z2), near + (S_2, S_ZM, S_ZP))
    arrived("px2p", "px2m")
    move(S_Z2)
    multiply_pairs(S_O, 2, 4, (S_Z2,))

    for s in step1 + step2:
        s.wait_send()
    for name in copies:
        copies[name].wait_send()


N_COPIES = 2 * 12 + 8 + 6 + 5


def gathered(taps, lags, counts):
    dma = pltpu.SemaphoreType.DMA
    return pl.pallas_call(
        gather_kernel,
        out_shape=jax.ShapeDtypeStruct((2, 8, 2048, 128), bf16),
        in_specs=[pl.BlockSpec(memory_space=pltpu.HBM)] * 3,
        out_specs=pl.BlockSpec(memory_space=pltpu.VMEM),
        scratch_shapes=[
            pltpu.SMEM((TAPS,), jnp.int32),
            pltpu.SMEM((2,), jnp.int32),
            pltpu.VMEM((ROWS, BINS), jnp.int32),
            pltpu.VMEM((9, ROWS, BINS), bf16),
            pltpu.VMEM((2048, BINS), bf16),
            pltpu.VMEM((8, BINS + LAGMAX, 128), bf16),
            pltpu.VMEM((8, BINS, 128), bf16),
            pltpu.VMEM((BINS + LAGMAX, 128), f32),
            pltpu.VMEM((ROWS, BINS), f32),
            pltpu.VMEM((BINS, 128), f32),
            pltpu.VMEM((8, BINS), f32),
            pltpu.VMEM((WIN, CH), bf16),
            pltpu.VMEM((CH, WIN), bf16),
            pltpu.VMEM((BINS, 128), bf16),
            pltpu.VMEM((1, BINS), f32),
            pltpu.VMEM((1, BINS), f32),
            pltpu.VMEM((7, 1, BINS), f32),
            pltpu.VMEM((15, 1, BINS), f32),
            dma((4,)), dma((7,)), dma((7,)), dma((15,)), dma((15,)),
            dma((N_COPIES,)), dma((N_COPIES,)),
        ],
        compiler_params=pltpu.CompilerParams(
            collective_id=0, has_side_effects=True, vmem_limit_bytes=44 << 20),
        name="gather_products",
    )(*(pltpu.with_memory_space_constraint(a, pltpu.HBM) for a in (taps, lags, counts)))


def layout_kernel(acc_ref, out_ref, buf, sem):
    rows, slots = buf.shape[1], buf.shape[0]
    steps = 2048 // rows
    puts = []
    for s in range(2 * steps):
        lag, first = s // steps, (s % steps) * rows
        if s >= slots:
            puts[s - slots].wait()
        buf[s % slots] = jnp.swapaxes(acc_ref[lag, :, first:first + rows, :].astype(f32), 0, 1).astype(bf16)
        put = pltpu.make_async_copy(buf.at[s % slots], out_ref.at[lag, first:first + rows], sem.at[s % slots])
        put.start()
        puts.append(put)
    for put in puts[-slots:]:
        put.wait()


def laid_out(acc):
    rows, slots = 256, 4
    return pl.pallas_call(
        layout_kernel,
        out_shape=jax.ShapeDtypeStruct((2, 2048, 8, 128), bf16),
        in_specs=[pl.BlockSpec(memory_space=pltpu.VMEM)],
        out_specs=pl.BlockSpec(memory_space=pl.ANY),
        scratch_shapes=[pltpu.VMEM((slots, rows, 8, 128), bf16), pltpu.SemaphoreType.DMA((slots,))],
        compiler_params=pltpu.CompilerParams(vmem_limit_bytes=24 << 20),
        name="layout",
    )(acc)


def shards(spike_counts, kernel_taps, lag_bins):
    return laid_out(gathered(kernel_taps, lag_bins, spike_counts))


def solution(mesh):
    placed = (P(("row", "blk"), None), P(), P())
    return jax.shard_map(
        shards, mesh=mesh, in_specs=placed, out_specs=P(None, "row", None, "blk"), check_vma=False
    )
```

```python
import functools

import jax
import jax.numpy as jnp
from jax import lax
from jax.experimental import pallas as pl
from jax.experimental.pallas import tpu as pltpu
from jax.sharding import PartitionSpec as P

NEURONS = 16384
BINS = 2048
TAPS = 16
LAGMAX = 32
MESH = pl.DeviceIdType.MESH
f32 = jnp.float32
bf16 = jnp.bfloat16

ROWS = 128
HALF = ROWS // 2
PAD = 128
CH = 256
NCH = BINS // CH
WIN = CH + PAD
QUARTER = ROWS // 4

O, XM, XP, X2, PZ, YM, YP, Y2, QZ = range(9)
S_O, S_Z, S_M, S_P, S_2, S_Z2, S_ZM, S_ZP = range(8)


def gather_kernel(taps_hbm, lag_hbm, counts_hbm, acc_ref,
                  taps_ref, lag_ref, counts, raw, bbuf, wz, ws, via, ft, fr, popt, popr, wrow, wcol, wsum,
                  own_sum, part_sum, got1, got2, lsem, snd1, rcv1, snd2, rcv2, ssem, rsem):
    row = lax.axis_index("row")
    blk = lax.axis_index("blk")
    zh, x = row // 4, row % 4
    zl, y, c = blk // 8, (blk // 2) % 4, blk % 2

    loads = [pltpu.make_async_copy(counts_hbm.at[h * HALF:(h + 1) * HALF, :],
                                   counts.at[h * HALF:(h + 1) * HALF, :], lsem.at[h]) for h in range(2)]
    loads += [pltpu.make_async_copy(taps_hbm, taps_ref, lsem.at[2]),
              pltpu.make_async_copy(lag_hbm, lag_ref, lsem.at[3])]
    for load in loads:
        load.start()

    def at(zh_, x_, zl_, y_, c_):
        return {"row": zh_ * 4 + x_, "blk": zl_ * 8 + y_ * 2 + c_}

    xp = at(zh, (x + 1) % 4, zl, y, c)
    xm = at(zh, (x + 3) % 4, zl, y, c)
    yp = at(zh, x, zl, (y + 1) % 4, c)
    ym = at(zh, x, zl, (y + 3) % 4, c)
    zq = at(zh, x, 1 - zl, y, c)
    zo = at(1 - zh, x, 1 - zl, y, c)
    cp = at(zh, x, zl, y, 1 - c)

    barrier = pltpu.get_barrier_semaphore()
    for d in range(1, 8):
        pl.semaphore_signal(barrier, inc=1, device_id={"row": (row + d) % 8, "blk": blk}, device_id_type=MESH)
    for d in range(1, 16):
        pl.semaphore_signal(barrier, inc=1, device_id={"row": row, "blk": (blk + d) % 16}, device_id_type=MESH)
    pl.semaphore_signal(barrier, inc=1, device_id=zo, device_id_type=MESH)

    for h in range(2):
        loads[h].wait()
        for n in range(NCH):
            part = counts[h * HALF:(h + 1) * HALF, n * CH:(n + 1) * CH].astype(f32)
            raw[O, h * HALF:(h + 1) * HALF, n * CH:(n + 1) * CH] = part.astype(bf16)
            part = jnp.sum(part, axis=0, keepdims=True)
            own_sum[:, n * CH:(n + 1) * CH] = part if h == 0 else own_sum[:, n * CH:(n + 1) * CH] + part
    pl.semaphore_wait(barrier, 23)

    step1 = [pltpu.make_async_remote_copy(
        src_ref=own_sum, dst_ref=got1.at[d - 1], send_sem=snd1.at[d - 1], recv_sem=rcv1.at[d - 1],
        device_id={"row": (row + d) % 8, "blk": blk}, device_id_type=MESH) for d in range(1, 8)]
    step2 = [pltpu.make_async_remote_copy(
        src_ref=part_sum, dst_ref=got2.at[d - 1], send_sem=snd2.at[d - 1], recv_sem=rcv2.at[d - 1],
        device_id={"row": row, "blk": (blk + d) % 16}, device_id_type=MESH) for d in range(1, 16)]

    copies = {}

    def copy(name, src, dst, device):
        k = len(copies)
        copies[name] = pltpu.make_async_remote_copy(
            src_ref=src, dst_ref=dst, send_sem=ssem.at[k], recv_sem=rsem.at[k],
            device_id=device, device_id_type=MESH)

    def start(*names):
        for name in names:
            copies[name].start()

    def arrived(*names):
        for name in names:
            copies[name].wait_recv()

    def raw_half(slot, h):
        return raw.at[slot, h * HALF:(h + 1) * HALF, :]

    def raw_quarter(slot, k):
        return raw.at[slot, k * QUARTER:(k + 1) * QUARTER, :]

    def wz_half(slot, h):
        return wz.at[slot, h * (BINS // 2):(h + 1) * (BINS // 2), :]

    def bb_half(slot, h, other=0):
        first = slot * 256 + other * ROWS + h * HALF
        return bbuf.at[first:first + HALF, :]

    def bb_rows(slot, first, size):
        return bbuf.at[slot * 256 + first:slot * 256 + first + size, :]

    for h in range(2):
        copy(("xp", h), raw_half(O, h), raw_half(XM, h), xp)
        copy(("xm", h), raw_half(O, h), raw_half(XP, h), xm)
        copy(("yp", h), raw_half(O, h), raw_half(YM, h), yp)
        copy(("ym", h), raw_half(O, h), raw_half(YP, h), ym)
        copy(("qyp", h), bb_half(S_Z, h), bb_half(S_ZM, h), yp)
        copy(("qym", h), bb_half(S_Z, h), bb_half(S_ZP, h), ym)
        for slot in (S_ZM, S_ZP):
            copy(("c", slot, h), bb_half(slot, h), bb_half(slot, h, 1), cp)
    for k in range(4):
        copy(("zq", k), raw_quarter(O, k), raw_quarter(QZ, k), zq)
        copy(("zo", k), raw_quarter(QZ, k), raw_quarter(PZ, k), zo)
    copy("x2p", raw_half(XM, 0), raw_half(X2, 0), xp)
    copy("x2m", raw_half(XP, 1), raw_half(X2, 1), xm)
    copy("y2p", raw_half(YM, 0), raw_half(Y2, 0), yp)
    copy("y2m", raw_half(YP, 1), raw_half(Y2, 1), ym)
    copy("a1", wz_half(S_M, 0), via.at[0], zq)
    copy("a2", via.at[0], wz_half(S_ZM, 0), zo)
    copy("b1", wz_half(S_P, 1), via.at[1], zo)
    copy("b2", via.at[1], wz_half(S_ZP, 1), zq)
    copy("pxp", wz_half(S_Z, 1), wz_half(S_ZM, 1), xp)
    copy("pxm", wz_half(S_Z, 0), wz_half(S_ZP, 0), xm)
    copy("px2p", wz_half(S_ZM, 1), wz_half(S_Z2, 1), xp)
    copy("px2m", wz_half(S_ZP, 0), wz_half(S_Z2, 0), xm)
    copy("qy2p", bb_rows(S_ZM, 0, QUARTER), bb_rows(S_Z2, 0, QUARTER), yp)
    copy("qy2m", bb_rows(S_ZP, 3 * QUARTER, QUARTER), bb_rows(S_Z2, 3 * QUARTER, QUARTER), ym)
    copy("zy", bb_rows(S_2, QUARTER, HALF), bb_rows(S_Z2, QUARTER, HALF), zq)
    for k, size in ((0, QUARTER), (QUARTER, HALF), (3 * QUARTER, QUARTER)):
        copy(("c", S_Z2, k), bb_rows(S_Z2, k, size), bb_rows(S_Z2, ROWS + k, size), cp)
    for slot in (S_O, S_Z, S_M, S_P, S_2):
        copy(("c", slot), bbuf.at[slot * 256:slot * 256 + ROWS, :],
             bbuf.at[slot * 256 + ROWS:slot * 256 + 2 * ROWS, :], cp)

    for s in step1:
        s.start()
    start(("zq", 0), ("xp", 0), ("xm", 1), ("yp", 0), ("ym", 1), ("zq", 1))

    loads[2].wait()
    loads[3].wait()
    taps = [taps_ref[k].astype(f32) for k in range(TAPS)]
    total = sum(taps[1:], taps[0])
    unit = 1.0 / jnp.full((8, 128), total, f32)
    late = lax.broadcasted_iota(jnp.int32, (WIN, CH), 1) + PAD - lax.broadcasted_iota(jnp.int32, (WIN, CH), 0)
    band = jnp.zeros((WIN, CH), f32)
    for k in range(TAPS):
        band = jnp.where(late == k, taps[k], band)
    wrow[...] = band.astype(bf16)
    late = lax.broadcasted_iota(jnp.int32, (CH, WIN), 0) + PAD - lax.broadcasted_iota(jnp.int32, (CH, WIN), 1)
    band = jnp.zeros((CH, WIN), f32)
    for k in range(TAPS):
        band = jnp.where(late == k, taps[k], band)
    wcol[...] = band.astype(bf16)
    wsum[...] = jnp.full((BINS, 128), total, f32).astype(bf16)
    left = TAPS - lax.broadcasted_iota(jnp.int32, (TAPS, 128), 0)
    edge = jnp.zeros((TAPS, 128), f32)
    for k in range(TAPS):
        edge = edge + jnp.where(left > k, taps[k], 0.0)
    wsum[BINS - TAPS:BINS, :] = edge.astype(bf16)
    ft[BINS:BINS + LAGMAX, :] = jnp.zeros((LAGMAX, 128), f32)
    for k in range(8):
        wz[k, BINS:BINS + LAGMAX, :] = jnp.zeros((LAGMAX, 128), bf16)

    for s in step1:
        s.wait_recv()
    part_sum[...] = own_sum[...] + sum([got1[d] for d in range(1, 7)], got1[0])
    for s in step2:
        s.start()
    start(("zq", 2), ("xp", 1), ("xm", 0), ("yp", 1), ("ym", 0), ("zq", 3))
    arrived(("zq", 0))
    start(("zo", 0))
    arrived(("xp", 0), ("xm", 1))
    start("x2p", "x2m")
    arrived(("yp", 0), ("ym", 1))
    start("y2p", "y2m")
    arrived(("zq", 1))
    start(("zo", 1))
    arrived(("zq", 2))
    start(("zo", 2))

    for s in step2:
        s.wait_recv()
    alls = part_sum[...] + sum([got2[d] for d in range(1, 15)], got2[0])
    high = alls.astype(bf16)
    rest = alls - high.astype(f32)
    mid = rest.astype(bf16)
    low = (rest - mid.astype(f32)).astype(bf16)
    summed = jnp.zeros((8, 128), f32)
    for n in range(NCH):
        first = max(n * CH - PAD, 0)
        wins = jnp.concatenate(
            [jnp.broadcast_to(piece[:, first:(n + 1) * CH], (16, (n + 1) * CH - first)) for piece in (high, mid, low)],
            axis=0)
        got = jnp.dot(wins, wrow[PAD:WIN, :] if n == 0 else wrow[...], preferred_element_type=f32)
        got = (got[0:8] + got[16:24]) + got[32:40]
        popr[:, n * CH:(n + 1) * CH] = got
        summed = summed + (got[:, 0:128] + got[:, 128:256])
    mean_pop = jnp.sum(summed, axis=1, keepdims=True) * (1.0 / BINS)
    popr[...] = (popr[...] - mean_pop) * (1.0 / NEURONS)
    for n in range(BINS // 128):
        popt[n * 128:(n + 1) * 128, :] = jnp.transpose(
            jnp.broadcast_to(popr[0:1, n * 128:(n + 1) * 128], (128, 128)))

    def to_rows(src, slot):
        mean = jnp.dot(raw[src], wsum[...], preferred_element_type=f32) * (1.0 / BINS)
        mean = jnp.concatenate([mean, mean], axis=1)
        q = jnp.zeros((ROWS, 128), f32)
        for n in range(NCH):
            if n == 0:
                got = jnp.dot(raw[src, :, 0:CH], wrow[PAD:WIN, :], preferred_element_type=f32)
            else:
                got = jnp.dot(raw[src, :, n * CH - PAD:(n + 1) * CH], wrow[...], preferred_element_type=f32)
            r = got - mean - popr[0:1, n * CH:(n + 1) * CH]
            fr[:, n * CH:(n + 1) * CH] = r
            r = r * r
            q = q + r[:, 0:128] + r[:, 128:256]
        u = unit[0:1, 0:1]
        scale = lax.rsqrt(jnp.sum(q, axis=1, keepdims=True) * (1.0 / BINS) * (u * u) + 1e-05) * u
        for n in range(NCH):
            bbuf[slot * 256:slot * 256 + ROWS, n * CH:(n + 1) * CH] = (
                fr[:, n * CH:(n + 1) * CH] * scale).astype(bf16)

    lag = lag_ref[0]

    def to_columns(src, slot):
        mean = jnp.transpose(jnp.dot(raw[src], wsum[...], preferred_element_type=f32) * (1.0 / BINS))[0:8]
        q = jnp.zeros((4, 8, 128), f32)
        for n in range(NCH):
            if n == 0:
                got = lax.dot_general(wcol[:, PAD:WIN], raw[src, :, 0:CH], (((1,), (1,)), ((), ())),
                                      preferred_element_type=f32)
            else:
                got = lax.dot_general(wcol[...], raw[src, :, n * CH - PAD:(n + 1) * CH], (((1,), (1,)), ((), ())),
                                      preferred_element_type=f32)
            r = got.reshape(32, 8, 128) - mean[None] - popt[n * CH:(n + 1) * CH, :].reshape(32, 8, 128)
            ft[n * CH:(n + 1) * CH, :] = r.reshape(CH, 128)
            r = r * r
            for j in range(8):
                q = q + r[4 * j:4 * j + 4]
        q = (q[0] + q[1]) + (q[2] + q[3])
        u = unit[0:1]
        scale = lax.rsqrt(jnp.sum(q, axis=0, keepdims=True) * (1.0 / BINS) * (u * u) + 1e-05) * u * (1.0 / BINS)
        for n in range(NCH):
            wz[slot, n * CH:(n + 1) * CH, :] = (ft[n * CH:(n + 1) * CH, :] * scale).astype(bf16)
            ws[slot, n * CH:(n + 1) * CH, :] = (ft[pl.ds(n * CH + lag, CH), :] * scale).astype(bf16)

    def move(slot):
        for n in range(NCH):
            ft[n * CH:(n + 1) * CH, :] = wz[slot, n * CH:(n + 1) * CH, :].astype(f32)
        for n in range(NCH):
            ws[slot, n * CH:(n + 1) * CH, :] = ft[pl.ds(n * CH + lag, CH), :].astype(bf16)

    def place(s, major, minor):
        j, i = s // 2, s % 2
        z = (major + i * ((j + 1) % 2) + j // 3) % 2
        return z * 4 + (minor + (j % 2) * (3 + 2 * i) + (j // 2) * (1 - j % 2) * 2) % 4

    def whole(s, pairs=1):
        return [(s * 256 + k * ROWS, ROWS, (place(s + k // 2, zl, y) * 2 + (c if k % 2 == 0 else 1 - c)) * ROWS)
                for k in range(2 * pairs)]

    def halves(s, h):
        return [(s * 256 + k * ROWS + h * HALF, HALF, (place(s, zl, y) * 2 + (c if k == 0 else 1 - c)) * ROWS + h * HALF)
                for k in range(2)]

    def multiply(segments, groups):
        runs = []
        for first, size, _ in segments:
            if runs and isinstance(first, int) and runs[-1][0] + runs[-1][1] == first:
                runs[-1][1] += size
            else:
                runs.append([first, size])
        left = [bbuf[first:first + size, :] if isinstance(first, int) else bbuf[pl.ds(first, size), :]
                for first, size in runs]
        left = left[0] if len(left) == 1 else jnp.concatenate(left, axis=0)
        for g in groups:
            right = jnp.concatenate([ws[g], wz[g, LAGMAX:LAGMAX + BINS, :]], axis=1)
            out = jnp.dot(left, right, preferred_element_type=f32)
            gg, k = place(g, zh, x), 0
            for _, size, there in segments:
                there = pl.ds(pl.multiple_of(there, size), size)
                acc_ref[0, gg, there, :] = out[k:k + size, 0:128].astype(bf16)
                acc_ref[1, gg, there, :] = out[k:k + size, 128:256].astype(bf16)
                k += size

    def multiply_pairs(first, count, pairs, groups):
        def one(n, _):
            s = first + n * pairs
            start_row = pl.multiple_of(s * 256, 256)
            left = bbuf[pl.ds(start_row, pairs * 256), :]
            for g in groups:
                right = jnp.concatenate([ws[g], wz[g, LAGMAX:LAGMAX + BINS, :]], axis=1)
                out = jnp.dot(left, right, preferred_element_type=f32)
                gg = place(g, zh, x)
                for k, (_, size, there) in enumerate(whole(s, pairs)):
                    there = pl.ds(pl.multiple_of(there, size), size)
                    acc_ref[0, gg, there, :] = out[k * size:(k + 1) * size, 0:128].astype(bf16)
                    acc_ref[1, gg, there, :] = out[k * size:(k + 1) * size, 128:256].astype(bf16)
            return 0
        lax.fori_loop(0, count, one, 0)

    near = (S_O, S_Z, S_M, S_P)
    early = halves(S_ZM, 0) + halves(S_ZP, 1)
    later = halves(S_ZM, 1) + halves(S_ZP, 0)
    to_rows(O, S_O)
    start(("c", S_O))
    arrived(("zq", 3))
    start(("zo", 3))
    to_rows(QZ, S_Z)
    start(("qyp", 0), ("qym", 1), ("qyp", 1), ("qym", 0), ("c", S_Z))
    arrived(("xp", 1), ("xm", 0))
    to_columns(XM, S_M)
    start("a1")
    to_columns(XP, S_P)
    start("b1")
    to_columns(O, S_O)
    arrived(("yp", 1), ("ym", 0))
    to_rows(YM, S_M)
    start(("c", S_M))
    arrived(("zo", 0), ("zo", 1), ("zo", 2), ("zo", 3))
    to_columns(PZ, S_Z)
    start("pxp", "pxm")
    to_rows(YP, S_P)
    start(("c", S_P))
    arrived("y2p", "y2m")
    to_rows(Y2, S_2)
    start("zy", ("c", S_2))
    arrived(("c", S_O), ("c", S_Z))
    multiply_pairs(S_O, 2, 1, near)
    arrived("x2p", "x2m")
    to_columns(X2, S_2)
    arrived("a1", "b1")
    start("a2", "b2")
    arrived(("c", S_M), ("c", S_P))
    multiply_pairs(S_M, 2, 1, near)
    arrived(("qyp", 0), ("qym", 1))
    start("qy2p", "qy2m", ("c", S_ZM, 0), ("c", S_ZP, 1))
    arrived("pxp", "pxm")
    start("px2p", "px2m")
    arrived(("c", S_2))
    multiply(whole(S_2), near)
    multiply(whole(S_O, 5), (S_2,))
    arrived(("c", S_ZM, 0), ("c", S_ZP, 1))
    multiply(early, near + (S_2,))
    arrived("a2")
    move(S_ZM)
    multiply(whole(S_O, 5) + early, (S_ZM,))
    arrived(("qyp", 1), ("qym", 0))
    start(("c", S_ZM, 1), ("c", S_ZP, 0))
    arrived("px2p", "px2m")
    move(S_Z2)
    multiply(whole(S_O, 5) + early, (S_Z2,))
    arrived("qy2p", "qy2m", "zy")
    start(("c", S_Z2, 0), ("c", S_Z2, 3 * QUARTER), ("c", S_Z2, QUARTER))
    arrived("b2")
    move(S_ZP)
    multiply(whole(S_O, 5) + early, (S_ZP,))
    arrived(("c", S_ZM, 1), ("c", S_ZP, 0))
    arrived(("c", S_Z2, 0), ("c", S_Z2, QUARTER), ("c", S_Z2, 3 * QUARTER))
    multiply(later + whole(S_Z2), near + (S_2, S_ZM, S_Z2, S_ZP))

    for s in step1 + step2:
        s.wait_send()
    for name in copies:
        copies[name].wait_send()


N_COPIES = 2 * 8 + 8 + 4 + 8 + 3 + 3 + 5


def gathered(taps, lags, counts):
    dma = pltpu.SemaphoreType.DMA
    return pl.pallas_call(
        gather_kernel,
        out_shape=jax.ShapeDtypeStruct((2, 8, 2048, 128), bf16),
        in_specs=[pl.BlockSpec(memory_space=pltpu.HBM)] * 3,
        out_specs=pl.BlockSpec(memory_space=pltpu.VMEM),
        scratch_shapes=[
            pltpu.SMEM((TAPS,), jnp.int32),
            pltpu.SMEM((2,), jnp.int32),
            pltpu.VMEM((ROWS, BINS), jnp.int32),
            pltpu.VMEM((9, ROWS, BINS), bf16),
            pltpu.VMEM((2048, BINS), bf16),
            pltpu.VMEM((8, BINS + LAGMAX, 128), bf16),
            pltpu.VMEM((8, BINS, 128), bf16),
            pltpu.VMEM((2, BINS // 2, 128), bf16),
            pltpu.VMEM((BINS + LAGMAX, 128), f32),
            pltpu.VMEM((ROWS, BINS), f32),
            pltpu.VMEM((BINS, 128), f32),
            pltpu.VMEM((8, BINS), f32),
            pltpu.VMEM((WIN, CH), bf16),
            pltpu.VMEM((CH, WIN), bf16),
            pltpu.VMEM((BINS, 128), bf16),
            pltpu.VMEM((1, BINS), f32),
            pltpu.VMEM((1, BINS), f32),
            pltpu.VMEM((7, 1, BINS), f32),
            pltpu.VMEM((15, 1, BINS), f32),
            dma((4,)), dma((7,)), dma((7,)), dma((15,)), dma((15,)),
            dma((N_COPIES,)), dma((N_COPIES,)),
        ],
        compiler_params=pltpu.CompilerParams(
            collective_id=0, has_side_effects=True, vmem_limit_bytes=44 << 20),
        name="gather_products",
    )(*(pltpu.with_memory_space_constraint(a, pltpu.HBM) for a in (taps, lags, counts)))


def layout_kernel(acc_ref, out_ref, buf, sem):
    rows, slots = buf.shape[1], buf.shape[0]
    steps = 2048 // rows
    puts = []
    for s in range(2 * steps):
        lag, first = s // steps, (s % steps) * rows
        if s >= slots:
            puts[s - slots].wait()
        buf[s % slots] = jnp.swapaxes(acc_ref[lag, :, first:first + rows, :].astype(f32), 0, 1).astype(bf16)
        put = pltpu.make_async_copy(buf.at[s % slots], out_ref.at[lag, first:first + rows], sem.at[s % slots])
        put.start()
        puts.append(put)
    for put in puts[-slots:]:
        put.wait()


def laid_out(acc):
    rows, slots = 256, 4
    return pl.pallas_call(
        layout_kernel,
        out_shape=jax.ShapeDtypeStruct((2, 2048, 8, 128), bf16),
        in_specs=[pl.BlockSpec(memory_space=pltpu.VMEM)],
        out_specs=pl.BlockSpec(memory_space=pl.ANY),
        scratch_shapes=[pltpu.VMEM((slots, rows, 8, 128), bf16), pltpu.SemaphoreType.DMA((slots,))],
        compiler_params=pltpu.CompilerParams(vmem_limit_bytes=24 << 20),
        name="layout",
    )(acc)


def shards(spike_counts, kernel_taps, lag_bins):
    return laid_out(gathered(kernel_taps, lag_bins, spike_counts))


def solution(mesh):
    placed = (P(("row", "blk"), None), P(), P())
    return jax.shard_map(
        shards, mesh=mesh, in_specs=placed, out_specs=P(None, "row", None, "blk"), check_vma=False
    )
```

```python
import functools

import jax
import jax.numpy as jnp
from jax import lax
from jax.experimental import pallas as pl
from jax.experimental.pallas import tpu as pltpu
from jax.sharding import PartitionSpec as P

NEURONS = 16384
BINS = 2048
TAPS = 16
LAGMAX = 32
MESH = pl.DeviceIdType.MESH
f32 = jnp.float32
bf16 = jnp.bfloat16

ROWS = 128
HALF = ROWS // 2
PAD = 128
CH = 256
NCH = BINS // CH
WIN = CH + PAD
QUARTER = ROWS // 4

O, XM, XP, X2, PZ, YM, YP, Y2, QZ = range(9)
S_O, S_Z, S_M, S_P, S_2, S_Z2, S_ZM, S_ZP = range(8)


def gather_kernel(taps_hbm, lag_hbm, counts_hbm, acc_ref,
                  taps_ref, lag_ref, counts, raw, bbuf, wz, ws, ft, fr, popt, popr, wrow, wcol, wsum,
                  own_sum, part_sum, got1, got2, lsem, snd1, rcv1, snd2, rcv2, ssem, rsem):
    row = lax.axis_index("row")
    blk = lax.axis_index("blk")
    zh, x = row // 4, row % 4
    zl, y, c = blk // 8, (blk // 2) % 4, blk % 2

    loads = [pltpu.make_async_copy(counts_hbm.at[h * HALF:(h + 1) * HALF, :],
                                   counts.at[h * HALF:(h + 1) * HALF, :], lsem.at[h]) for h in range(2)]
    loads += [pltpu.make_async_copy(taps_hbm, taps_ref, lsem.at[2]),
              pltpu.make_async_copy(lag_hbm, lag_ref, lsem.at[3])]
    for load in loads:
        load.start()

    def at(zh_, x_, zl_, y_, c_):
        return {"row": zh_ * 4 + x_, "blk": zl_ * 8 + y_ * 2 + c_}

    xp = at(zh, (x + 1) % 4, zl, y, c)
    xm = at(zh, (x + 3) % 4, zl, y, c)
    yp = at(zh, x, zl, (y + 1) % 4, c)
    ym = at(zh, x, zl, (y + 3) % 4, c)
    zq = at(zh, x, 1 - zl, y, c)
    zo = at(1 - zh, x, 1 - zl, y, c)
    cp = at(zh, x, zl, y, 1 - c)

    barrier = pltpu.get_barrier_semaphore()
    for d in range(1, 8):
        pl.semaphore_signal(barrier, inc=1, device_id={"row": (row + d) % 8, "blk": blk}, device_id_type=MESH)
    for d in range(1, 16):
        pl.semaphore_signal(barrier, inc=1, device_id={"row": row, "blk": (blk + d) % 16}, device_id_type=MESH)
    pl.semaphore_signal(barrier, inc=1, device_id=zo, device_id_type=MESH)

    for h in range(2):
        loads[h].wait()
        for n in range(NCH):
            part = counts[h * HALF:(h + 1) * HALF, n * CH:(n + 1) * CH].astype(f32)
            raw[O, h * HALF:(h + 1) * HALF, n * CH:(n + 1) * CH] = part.astype(bf16)
            part = jnp.sum(part, axis=0, keepdims=True)
            own_sum[:, n * CH:(n + 1) * CH] = part if h == 0 else own_sum[:, n * CH:(n + 1) * CH] + part
    pl.semaphore_wait(barrier, 23)

    step1 = [pltpu.make_async_remote_copy(
        src_ref=own_sum, dst_ref=got1.at[d - 1], send_sem=snd1.at[d - 1], recv_sem=rcv1.at[d - 1],
        device_id={"row": (row + d) % 8, "blk": blk}, device_id_type=MESH) for d in range(1, 8)]
    step2 = [pltpu.make_async_remote_copy(
        src_ref=part_sum, dst_ref=got2.at[d - 1], send_sem=snd2.at[d - 1], recv_sem=rcv2.at[d - 1],
        device_id={"row": row, "blk": (blk + d) % 16}, device_id_type=MESH) for d in range(1, 16)]

    copies = {}

    def copy(name, src, dst, device):
        k = len(copies)
        copies[name] = pltpu.make_async_remote_copy(
            src_ref=src, dst_ref=dst, send_sem=ssem.at[k], recv_sem=rsem.at[k],
            device_id=device, device_id_type=MESH)

    def start(*names):
        for name in names:
            copies[name].start()

    def arrived(*names):
        for name in names:
            copies[name].wait_recv()

    def raw_half(slot, h):
        return raw.at[slot, h * HALF:(h + 1) * HALF, :]

    def raw_quarter(slot, k):
        return raw.at[slot, k * QUARTER:(k + 1) * QUARTER, :]

    def wz_half(slot, h):
        return wz.at[slot, h * (BINS // 2):(h + 1) * (BINS // 2), :]

    def bb_half(slot, h, other=0):
        first = slot * 256 + other * ROWS + h * HALF
        return bbuf.at[first:first + HALF, :]

    for h in range(2):
        copy(("xp", h), raw_half(O, h), raw_half(XM, h), xp)
        copy(("xm", h), raw_half(O, h), raw_half(XP, h), xm)
        copy(("yp", h), raw_half(O, h), raw_half(YM, h), yp)
        copy(("ym", h), raw_half(O, h), raw_half(YP, h), ym)
        copy(("pxp", h), wz_half(S_Z, h), wz_half(S_ZM, h), xp)
        copy(("pxm", h), wz_half(S_Z, h), wz_half(S_ZP, h), xm)
        copy(("qyp", h), bb_half(S_Z, h), bb_half(S_ZM, h), yp)
        copy(("qym", h), bb_half(S_Z, h), bb_half(S_ZP, h), ym)
        copy(("zy", h), bb_half(S_2, h), bb_half(S_Z2, h), zq)
        for slot in (S_Z2, S_ZM, S_ZP):
            copy(("c", slot, h), bb_half(slot, h), bb_half(slot, h, 1), cp)
    for k in range(4):
        copy(("zq", k), raw_quarter(O, k), raw_quarter(QZ, k), zq)
        copy(("zo", k), raw_quarter(QZ, k), raw_quarter(PZ, k), zo)
    copy("x2p", raw_half(XM, 0), raw_half(X2, 0), xp)
    copy("x2m", raw_half(XP, 1), raw_half(X2, 1), xm)
    copy("y2p", raw_half(YM, 0), raw_half(Y2, 0), yp)
    copy("y2m", raw_half(YP, 1), raw_half(Y2, 1), ym)
    copy("px2p", wz_half(S_ZM, 0), wz_half(S_Z2, 0), xp)
    copy("px2m", wz_half(S_ZP, 1), wz_half(S_Z2, 1), xm)
    for slot in (S_O, S_Z, S_M, S_P, S_2):
        copy(("c", slot), bbuf.at[slot * 256:slot * 256 + ROWS, :],
             bbuf.at[slot * 256 + ROWS:slot * 256 + 2 * ROWS, :], cp)

    for s in step1:
        s.start()
    start(("zq", 0), ("xp", 0), ("xm", 1), ("yp", 0), ("ym", 1), ("zq", 1))

    loads[2].wait()
    loads[3].wait()
    taps = [taps_ref[k].astype(f32) for k in range(TAPS)]
    total = sum(taps[1:], taps[0])
    unit = 1.0 / jnp.full((8, 128), total, f32)
    late = lax.broadcasted_iota(jnp.int32, (WIN, CH), 1) + PAD - lax.broadcasted_iota(jnp.int32, (WIN, CH), 0)
    band = jnp.zeros((WIN, CH), f32)
    for k in range(TAPS):
        band = jnp.where(late == k, taps[k], band)
    wrow[...] = band.astype(bf16)
    late = lax.broadcasted_iota(jnp.int32, (CH, WIN), 0) + PAD - lax.broadcasted_iota(jnp.int32, (CH, WIN), 1)
    band = jnp.zeros((CH, WIN), f32)
    for k in range(TAPS):
        band = jnp.where(late == k, taps[k], band)
    wcol[...] = band.astype(bf16)
    wsum[...] = jnp.full((BINS, 128), total, f32).astype(bf16)
    left = TAPS - lax.broadcasted_iota(jnp.int32, (TAPS, 128), 0)
    edge = jnp.zeros((TAPS, 128), f32)
    for k in range(TAPS):
        edge = edge + jnp.where(left > k, taps[k], 0.0)
    wsum[BINS - TAPS:BINS, :] = edge.astype(bf16)
    ft[BINS:BINS + LAGMAX, :] = jnp.zeros((LAGMAX, 128), f32)
    for k in range(8):
        wz[k, BINS:BINS + LAGMAX, :] = jnp.zeros((LAGMAX, 128), bf16)

    for s in step1:
        s.wait_recv()
    part_sum[...] = own_sum[...] + sum([got1[d] for d in range(1, 7)], got1[0])
    for s in step2:
        s.start()
    start(("zq", 2), ("xp", 1), ("xm", 0), ("yp", 1), ("ym", 0), ("zq", 3))
    arrived(("zq", 0))
    start(("zo", 0))
    arrived(("xp", 0), ("xm", 1))
    start("x2p", "x2m")
    arrived(("yp", 0), ("ym", 1))
    start("y2p", "y2m")
    arrived(("zq", 1))
    start(("zo", 1))
    arrived(("zq", 2))
    start(("zo", 2))

    for s in step2:
        s.wait_recv()
    alls = part_sum[...] + sum([got2[d] for d in range(1, 15)], got2[0])
    high = alls.astype(bf16)
    rest = alls - high.astype(f32)
    mid = rest.astype(bf16)
    low = (rest - mid.astype(f32)).astype(bf16)
    summed = jnp.zeros((8, 128), f32)
    for n in range(NCH):
        first = max(n * CH - PAD, 0)
        wins = jnp.concatenate(
            [jnp.broadcast_to(piece[:, first:(n + 1) * CH], (16, (n + 1) * CH - first)) for piece in (high, mid, low)],
            axis=0)
        got = jnp.dot(wins, wrow[PAD:WIN, :] if n == 0 else wrow[...], preferred_element_type=f32)
        got = (got[0:8] + got[16:24]) + got[32:40]
        popr[:, n * CH:(n + 1) * CH] = got
        summed = summed + (got[:, 0:128] + got[:, 128:256])
    mean_pop = jnp.sum(summed, axis=1, keepdims=True) * (1.0 / BINS)
    popr[...] = (popr[...] - mean_pop) * (1.0 / NEURONS)
    for n in range(BINS // 128):
        popt[n * 128:(n + 1) * 128, :] = jnp.transpose(
            jnp.broadcast_to(popr[0:1, n * 128:(n + 1) * 128], (128, 128)))

    def to_rows(src, slot):
        mean = jnp.dot(raw[src], wsum[...], preferred_element_type=f32) * (1.0 / BINS)
        mean = jnp.concatenate([mean, mean], axis=1)
        q = jnp.zeros((ROWS, 128), f32)
        for n in range(NCH):
            if n == 0:
                got = jnp.dot(raw[src, :, 0:CH], wrow[PAD:WIN, :], preferred_element_type=f32)
            else:
                got = jnp.dot(raw[src, :, n * CH - PAD:(n + 1) * CH], wrow[...], preferred_element_type=f32)
            r = got - mean - popr[0:1, n * CH:(n + 1) * CH]
            fr[:, n * CH:(n + 1) * CH] = r
            r = r * r
            q = q + r[:, 0:128] + r[:, 128:256]
        u = unit[0:1, 0:1]
        scale = lax.rsqrt(jnp.sum(q, axis=1, keepdims=True) * (1.0 / BINS) * (u * u) + 1e-05) * u
        for n in range(NCH):
            bbuf[slot * 256:slot * 256 + ROWS, n * CH:(n + 1) * CH] = (
                fr[:, n * CH:(n + 1) * CH] * scale).astype(bf16)

    lag = lag_ref[0]

    def to_columns(src, slot):
        mean = jnp.transpose(jnp.dot(raw[src], wsum[...], preferred_element_type=f32) * (1.0 / BINS))[0:8]
        q = jnp.zeros((4, 8, 128), f32)
        for n in range(NCH):
            if n == 0:
                got = lax.dot_general(wcol[:, PAD:WIN], raw[src, :, 0:CH], (((1,), (1,)), ((), ())),
                                      preferred_element_type=f32)
            else:
                got = lax.dot_general(wcol[...], raw[src, :, n * CH - PAD:(n + 1) * CH], (((1,), (1,)), ((), ())),
                                      preferred_element_type=f32)
            r = got.reshape(32, 8, 128) - mean[None] - popt[n * CH:(n + 1) * CH, :].reshape(32, 8, 128)
            ft[n * CH:(n + 1) * CH, :] = r.reshape(CH, 128)
            r = r * r
            for j in range(8):
                q = q + r[4 * j:4 * j + 4]
        q = (q[0] + q[1]) + (q[2] + q[3])
        u = unit[0:1]
        scale = lax.rsqrt(jnp.sum(q, axis=0, keepdims=True) * (1.0 / BINS) * (u * u) + 1e-05) * u * (1.0 / BINS)
        for n in range(NCH):
            wz[slot, n * CH:(n + 1) * CH, :] = (ft[n * CH:(n + 1) * CH, :] * scale).astype(bf16)
            ws[slot, n * CH:(n + 1) * CH, :] = (ft[pl.ds(n * CH + lag, CH), :] * scale).astype(bf16)

    def move(slot):
        for n in range(NCH):
            ft[n * CH:(n + 1) * CH, :] = wz[slot, n * CH:(n + 1) * CH, :].astype(f32)
        for n in range(NCH):
            ws[slot, n * CH:(n + 1) * CH, :] = ft[pl.ds(n * CH + lag, CH), :].astype(bf16)

    def place(s, major, minor):
        j, i = s // 2, s % 2
        z = (major + i * ((j + 1) % 2) + j // 3) % 2
        return z * 4 + (minor + (j % 2) * (3 + 2 * i) + (j // 2) * (1 - j % 2) * 2) % 4

    def whole(s, pairs=1):
        return [(s * 256 + k * ROWS, ROWS, (place(s + k // 2, zl, y) * 2 + (c if k % 2 == 0 else 1 - c)) * ROWS)
                for k in range(2 * pairs)]

    def halves(s, h):
        return [(s * 256 + k * ROWS + h * HALF, HALF, (place(s, zl, y) * 2 + (c if k == 0 else 1 - c)) * ROWS + h * HALF)
                for k in range(2)]

    def multiply(segments, groups):
        runs = []
        for first, size, _ in segments:
            if runs and isinstance(first, int) and runs[-1][0] + runs[-1][1] == first:
                runs[-1][1] += size
            else:
                runs.append([first, size])
        left = [bbuf[first:first + size, :] if isinstance(first, int) else bbuf[pl.ds(first, size), :]
                for first, size in runs]
        left = left[0] if len(left) == 1 else jnp.concatenate(left, axis=0)
        for g in groups:
            right = jnp.concatenate([ws[g], wz[g, LAGMAX:LAGMAX + BINS, :]], axis=1)
            out = jnp.dot(left, right, preferred_element_type=f32)
            gg, k = place(g, zh, x), 0
            for _, size, there in segments:
                there = pl.ds(pl.multiple_of(there, size), size)
                acc_ref[0, gg, there, :] = out[k:k + size, 0:128].astype(bf16)
                acc_ref[1, gg, there, :] = out[k:k + size, 128:256].astype(bf16)
                k += size

    def multiply_pairs(first, count, pairs, groups):
        def one(n, _):
            s = first + n * pairs
            start_row = pl.multiple_of(s * 256, 256)
            left = bbuf[pl.ds(start_row, pairs * 256), :]
            for g in groups:
                right = jnp.concatenate([ws[g], wz[g, LAGMAX:LAGMAX + BINS, :]], axis=1)
                out = jnp.dot(left, right, preferred_element_type=f32)
                gg = place(g, zh, x)
                for k, (_, size, there) in enumerate(whole(s, pairs)):
                    there = pl.ds(pl.multiple_of(there, size), size)
                    acc_ref[0, gg, there, :] = out[k * size:(k + 1) * size, 0:128].astype(bf16)
                    acc_ref[1, gg, there, :] = out[k * size:(k + 1) * size, 128:256].astype(bf16)
            return 0
        lax.fori_loop(0, count, one, 0)

    near = (S_O, S_Z, S_M, S_P)
    to_rows(O, S_O)
    start(("c", S_O))
    arrived(("zq", 3))
    start(("zo", 3))
    to_rows(QZ, S_Z)
    start(("qyp", 0), ("qym", 1), ("qyp", 1), ("qym", 0), ("c", S_Z))
    to_columns(O, S_O)
    arrived(("xp", 1), ("xm", 0), ("yp", 1), ("ym", 0))
    to_columns(XM, S_M)
    to_columns(XP, S_P)
    to_rows(YM, S_M)
    start(("c", S_M))
    arrived(("zo", 0), ("zo", 1), ("zo", 2), ("zo", 3))
    to_columns(PZ, S_Z)
    start(("pxp", 0), ("pxm", 1), ("pxp", 1), ("pxm", 0))
    to_rows(YP, S_P)
    start(("c", S_P))
    arrived("y2p", "y2m")
    to_rows(Y2, S_2)
    start(("zy", 0), ("zy", 1), ("c", S_2))
    arrived(("c", S_O), ("c", S_Z))
    multiply_pairs(S_O, 2, 1, near)
    arrived("x2p", "x2m")
    to_columns(X2, S_2)
    arrived(("c", S_M), ("c", S_P), ("c", S_2))
    multiply_pairs(S_M, 3, 1, near)
    arrived(("qyp", 0), ("qym", 1))
    start(("c", S_ZM, 0), ("c", S_ZP, 1))
    arrived(("pxp", 0), ("pxm", 1))
    start("px2p", "px2m")
    multiply(whole(S_O, 5), (S_2,))
    early = halves(S_ZM, 0) + halves(S_ZP, 1)
    later = halves(S_ZM, 1) + halves(S_ZP, 0)
    arrived(("c", S_ZM, 0), ("c", S_ZP, 1))
    multiply(early, near + (S_2,))
    arrived(("qyp", 1), ("qym", 0))
    start(("c", S_ZM, 1), ("c", S_ZP, 0))
    arrived(("pxp", 1), ("pxm", 0))
    move(S_ZM)
    move(S_ZP)
    multiply(whole(S_O, 4), (S_ZM, S_ZP))
    arrived(("zy", 0), ("zy", 1))
    start(("c", S_Z2, 0), ("c", S_Z2, 1))
    multiply(whole(S_2) + early, (S_ZM, S_ZP))
    arrived(("c", S_ZM, 1), ("c", S_ZP, 0))
    arrived(("c", S_Z2, 0), ("c", S_Z2, 1))
    multiply(later + whole(S_Z2), near + (S_2, S_ZM, S_ZP))
    arrived("px2p", "px2m")
    move(S_Z2)
    multiply(whole(S_O, 8), (S_Z2,))

    for s in step1 + step2:
        s.wait_send()
    for name in copies:
        copies[name].wait_send()


N_COPIES = 2 * 12 + 8 + 6 + 5


def gathered(taps, lags, counts):
    dma = pltpu.SemaphoreType.DMA
    return pl.pallas_call(
        gather_kernel,
        out_shape=jax.ShapeDtypeStruct((2, 8, 2048, 128), bf16),
        in_specs=[pl.BlockSpec(memory_space=pltpu.HBM)] * 3,
        out_specs=pl.BlockSpec(memory_space=pltpu.VMEM),
        scratch_shapes=[
            pltpu.SMEM((TAPS,), jnp.int32),
            pltpu.SMEM((2,), jnp.int32),
            pltpu.VMEM((ROWS, BINS), jnp.int32),
            pltpu.VMEM((9, ROWS, BINS), bf16),
            pltpu.VMEM((2048, BINS), bf16),
            pltpu.VMEM((8, BINS + LAGMAX, 128), bf16),
            pltpu.VMEM((8, BINS, 128), bf16),
            pltpu.VMEM((BINS + LAGMAX, 128), f32),
            pltpu.VMEM((ROWS, BINS), f32),
            pltpu.VMEM((BINS, 128), f32),
            pltpu.VMEM((8, BINS), f32),
            pltpu.VMEM((WIN, CH), bf16),
            pltpu.VMEM((CH, WIN), bf16),
            pltpu.VMEM((BINS, 128), bf16),
            pltpu.VMEM((1, BINS), f32),
            pltpu.VMEM((1, BINS), f32),
            pltpu.VMEM((7, 1, BINS), f32),
            pltpu.VMEM((15, 1, BINS), f32),
            dma((4,)), dma((7,)), dma((7,)), dma((15,)), dma((15,)),
            dma((N_COPIES,)), dma((N_COPIES,)),
        ],
        compiler_params=pltpu.CompilerParams(
            collective_id=0, has_side_effects=True, vmem_limit_bytes=44 << 20),
        name="gather_products",
    )(*(pltpu.with_memory_space_constraint(a, pltpu.HBM) for a in (taps, lags, counts)))


def layout_kernel(acc_ref, out_ref, buf, sem):
    rows, slots = buf.shape[1], buf.shape[0]
    steps = 2048 // rows
    puts = []
    for s in range(2 * steps):
        lag, first = s // steps, (s % steps) * rows
        if s >= slots:
            puts[s - slots].wait()
        buf[s % slots] = jnp.swapaxes(acc_ref[lag, :, first:first + rows, :], 0, 1)
        put = pltpu.make_async_copy(buf.at[s % slots], out_ref.at[lag, first:first + rows], sem.at[s % slots])
        put.start()
        puts.append(put)
    for put in puts[-slots:]:
        put.wait()


def laid_out(acc):
    rows, slots = 256, 8
    return pl.pallas_call(
        layout_kernel,
        out_shape=jax.ShapeDtypeStruct((2, 2048, 8, 128), bf16),
        in_specs=[pl.BlockSpec(memory_space=pltpu.VMEM)],
        out_specs=pl.BlockSpec(memory_space=pl.ANY),
        scratch_shapes=[pltpu.VMEM((slots, rows, 8, 128), bf16), pltpu.SemaphoreType.DMA((slots,))],
        compiler_params=pltpu.CompilerParams(vmem_limit_bytes=24 << 20),
        name="layout",
    )(acc)


def shards(spike_counts, kernel_taps, lag_bins):
    return laid_out(gathered(kernel_taps, lag_bins, spike_counts))


def solution(mesh):
    placed = (P(("row", "blk"), None), P(), P())
    return jax.shard_map(
        shards, mesh=mesh, in_specs=placed, out_specs=P(None, "row", None, "blk"), check_vma=False
    )
```

```python
import functools

import jax
import jax.numpy as jnp
from jax import lax
from jax.experimental import pallas as pl
from jax.experimental.pallas import tpu as pltpu
from jax.sharding import PartitionSpec as P

NEURONS = 16384
BINS = 2048
TAPS = 16
LAGMAX = 32
MESH = pl.DeviceIdType.MESH
f32 = jnp.float32
bf16 = jnp.bfloat16

ROWS = 128
HALF = ROWS // 2
PAD = 128
CH = 256
NCH = BINS // CH
WIN = CH + PAD
QUARTER = ROWS // 4

O, XM, XP, X2, PZ, YM, YP, Y2, QZ = range(9)
S_O, S_Z, S_M, S_P, S_2, S_Z2, S_ZM, S_ZP = range(8)


def gather_kernel(taps_hbm, lag_hbm, counts_hbm, acc_ref,
                  taps_ref, lag_ref, counts, raw, bbuf, wz, ws, ft, fr, popt, popr, wrow, wcol, wsum,
                  own_sum, part_sum, got1, got2, lsem, snd1, rcv1, snd2, rcv2, ssem, rsem):
    row = lax.axis_index("row")
    blk = lax.axis_index("blk")
    zh, x = row // 4, row % 4
    zl, y, c = blk // 8, (blk // 2) % 4, blk % 2

    loads = [pltpu.make_async_copy(counts_hbm.at[h * HALF:(h + 1) * HALF, :],
                                   counts.at[h * HALF:(h + 1) * HALF, :], lsem.at[h]) for h in range(2)]
    loads += [pltpu.make_async_copy(taps_hbm, taps_ref, lsem.at[2]),
              pltpu.make_async_copy(lag_hbm, lag_ref, lsem.at[3])]
    for load in loads:
        load.start()

    def at(zh_, x_, zl_, y_, c_):
        return {"row": zh_ * 4 + x_, "blk": zl_ * 8 + y_ * 2 + c_}

    xp = at(zh, (x + 1) % 4, zl, y, c)
    xm = at(zh, (x + 3) % 4, zl, y, c)
    yp = at(zh, x, zl, (y + 1) % 4, c)
    ym = at(zh, x, zl, (y + 3) % 4, c)
    zq = at(zh, x, 1 - zl, y, c)
    zo = at(1 - zh, x, 1 - zl, y, c)
    cp = at(zh, x, zl, y, 1 - c)

    barrier = pltpu.get_barrier_semaphore()
    for d in range(1, 8):
        pl.semaphore_signal(barrier, inc=1, device_id={"row": (row + d) % 8, "blk": blk}, device_id_type=MESH)
    for d in range(1, 16):
        pl.semaphore_signal(barrier, inc=1, device_id={"row": row, "blk": (blk + d) % 16}, device_id_type=MESH)
    pl.semaphore_signal(barrier, inc=1, device_id=zo, device_id_type=MESH)

    for h in range(2):
        loads[h].wait()
        for n in range(NCH):
            part = counts[h * HALF:(h + 1) * HALF, n * CH:(n + 1) * CH].astype(f32)
            raw[O, h * HALF:(h + 1) * HALF, n * CH:(n + 1) * CH] = part.astype(bf16)
            part = jnp.sum(part, axis=0, keepdims=True)
            own_sum[:, n * CH:(n + 1) * CH] = part if h == 0 else own_sum[:, n * CH:(n + 1) * CH] + part
    pl.semaphore_wait(barrier, 23)

    step1 = [pltpu.make_async_remote_copy(
        src_ref=own_sum, dst_ref=got1.at[d - 1], send_sem=snd1.at[d - 1], recv_sem=rcv1.at[d - 1],
        device_id={"row": (row + d) % 8, "blk": blk}, device_id_type=MESH) for d in range(1, 8)]
    step2 = [pltpu.make_async_remote_copy(
        src_ref=part_sum, dst_ref=got2.at[d - 1], send_sem=snd2.at[d - 1], recv_sem=rcv2.at[d - 1],
        device_id={"row": row, "blk": (blk + d) % 16}, device_id_type=MESH) for d in range(1, 16)]

    copies = {}

    def copy(name, src, dst, device):
        k = len(copies)
        copies[name] = pltpu.make_async_remote_copy(
            src_ref=src, dst_ref=dst, send_sem=ssem.at[k], recv_sem=rsem.at[k],
            device_id=device, device_id_type=MESH)

    def start(*names):
        for name in names:
            copies[name].start()

    def arrived(*names):
        for name in names:
            copies[name].wait_recv()

    def raw_half(slot, h):
        return raw.at[slot, h * HALF:(h + 1) * HALF, :]

    def raw_quarter(slot, k):
        return raw.at[slot, k * QUARTER:(k + 1) * QUARTER, :]

    def wz_half(slot, h):
        return wz.at[slot, h * (BINS // 2):(h + 1) * (BINS // 2), :]

    def bb_half(slot, h, other=0):
        first = slot * 256 + other * ROWS + h * HALF
        return bbuf.at[first:first + HALF, :]

    for h in range(2):
        copy(("xp", h), raw_half(O, h), raw_half(XM, h), xp)
        copy(("xm", h), raw_half(O, h), raw_half(XP, h), xm)
        copy(("yp", h), raw_half(O, h), raw_half(YM, h), yp)
        copy(("ym", h), raw_half(O, h), raw_half(YP, h), ym)
        copy(("pxp", h), wz_half(S_Z, h), wz_half(S_ZM, h), xp)
        copy(("pxm", h), wz_half(S_Z, h), wz_half(S_ZP, h), xm)
        copy(("qyp", h), bb_half(S_Z, h), bb_half(S_ZM, h), yp)
        copy(("qym", h), bb_half(S_Z, h), bb_half(S_ZP, h), ym)
        copy(("zy", h), bb_half(S_2, h), bb_half(S_Z2, h), zq)
        for slot in (S_Z2, S_ZM, S_ZP):
            copy(("c", slot, h), bb_half(slot, h), bb_half(slot, h, 1), cp)
    for k in range(4):
        copy(("zq", k), raw_quarter(O, k), raw_quarter(QZ, k), zq)
        copy(("zo", k), raw_quarter(QZ, k), raw_quarter(PZ, k), zo)
    copy("x2p", raw_half(XM, 0), raw_half(X2, 0), xp)
    copy("x2m", raw_half(XP, 1), raw_half(X2, 1), xm)
    copy("y2p", raw_half(YM, 0), raw_half(Y2, 0), yp)
    copy("y2m", raw_half(YP, 1), raw_half(Y2, 1), ym)
    copy("px2p", wz_half(S_ZM, 0), wz_half(S_Z2, 0), xp)
    copy("px2m", wz_half(S_ZP, 1), wz_half(S_Z2, 1), xm)
    for slot in (S_O, S_Z, S_M, S_P, S_2):
        copy(("c", slot), bbuf.at[slot * 256:slot * 256 + ROWS, :],
             bbuf.at[slot * 256 + ROWS:slot * 256 + 2 * ROWS, :], cp)

    for s in step1:
        s.start()
    start(("zq", 0), ("xp", 0), ("xm", 1), ("yp", 0), ("ym", 1), ("zq", 1))

    loads[2].wait()
    loads[3].wait()
    taps = [taps_ref[k].astype(f32) for k in range(TAPS)]
    total = sum(taps[1:], taps[0])
    unit = 1.0 / jnp.full((8, 128), total, f32)
    late = lax.broadcasted_iota(jnp.int32, (WIN, CH), 1) + PAD - lax.broadcasted_iota(jnp.int32, (WIN, CH), 0)
    band = jnp.zeros((WIN, CH), f32)
    for k in range(TAPS):
        band = jnp.where(late == k, taps[k], band)
    wrow[...] = band.astype(bf16)
    late = lax.broadcasted_iota(jnp.int32, (CH, WIN), 0) + PAD - lax.broadcasted_iota(jnp.int32, (CH, WIN), 1)
    band = jnp.zeros((CH, WIN), f32)
    for k in range(TAPS):
        band = jnp.where(late == k, taps[k], band)
    wcol[...] = band.astype(bf16)
    wsum[...] = jnp.full((BINS, 128), total, f32).astype(bf16)
    left = TAPS - lax.broadcasted_iota(jnp.int32, (TAPS, 128), 0)
    edge = jnp.zeros((TAPS, 128), f32)
    for k in range(TAPS):
        edge = edge + jnp.where(left > k, taps[k], 0.0)
    wsum[BINS - TAPS:BINS, :] = edge.astype(bf16)
    ft[BINS:BINS + LAGMAX, :] = jnp.zeros((LAGMAX, 128), f32)
    for k in range(8):
        wz[k, BINS:BINS + LAGMAX, :] = jnp.zeros((LAGMAX, 128), bf16)

    for s in step1:
        s.wait_recv()
    part_sum[...] = own_sum[...] + sum([got1[d] for d in range(1, 7)], got1[0])
    for s in step2:
        s.start()
    start(("zq", 2), ("xp", 1), ("xm", 0), ("yp", 1), ("ym", 0), ("zq", 3))
    arrived(("zq", 0))
    start(("zo", 0))
    arrived(("xp", 0), ("xm", 1))
    start("x2p", "x2m")
    arrived(("yp", 0), ("ym", 1))
    start("y2p", "y2m")
    arrived(("zq", 1))
    start(("zo", 1))
    arrived(("zq", 2))
    start(("zo", 2))

    for s in step2:
        s.wait_recv()
    alls = part_sum[...] + sum([got2[d] for d in range(1, 15)], got2[0])
    high = alls.astype(bf16)
    rest = alls - high.astype(f32)
    mid = rest.astype(bf16)
    low = (rest - mid.astype(f32)).astype(bf16)
    summed = jnp.zeros((8, 128), f32)
    for n in range(NCH):
        first = max(n * CH - PAD, 0)
        wins = jnp.concatenate(
            [jnp.broadcast_to(piece[:, first:(n + 1) * CH], (16, (n + 1) * CH - first)) for piece in (high, mid, low)],
            axis=0)
        got = jnp.dot(wins, wrow[PAD:WIN, :] if n == 0 else wrow[...], preferred_element_type=f32)
        got = (got[0:8] + got[16:24]) + got[32:40]
        popr[:, n * CH:(n + 1) * CH] = got
        summed = summed + (got[:, 0:128] + got[:, 128:256])
    mean_pop = jnp.sum(summed, axis=1, keepdims=True) * (1.0 / BINS)
    popr[...] = (popr[...] - mean_pop) * (1.0 / NEURONS)
    for n in range(BINS // 128):
        popt[n * 128:(n + 1) * 128, :] = jnp.transpose(
            jnp.broadcast_to(popr[0:1, n * 128:(n + 1) * 128], (128, 128)))

    def to_rows(src, slot):
        mean = jnp.dot(raw[src], wsum[...], preferred_element_type=f32) * (1.0 / BINS)
        mean = jnp.concatenate([mean, mean], axis=1)
        q = jnp.zeros((ROWS, 128), f32)
        for n in range(NCH):
            if n == 0:
                got = jnp.dot(raw[src, :, 0:CH], wrow[PAD:WIN, :], preferred_element_type=f32)
            else:
                got = jnp.dot(raw[src, :, n * CH - PAD:(n + 1) * CH], wrow[...], preferred_element_type=f32)
            r = got - mean - popr[0:1, n * CH:(n + 1) * CH]
            fr[:, n * CH:(n + 1) * CH] = r
            r = r * r
            q = q + r[:, 0:128] + r[:, 128:256]
        u = unit[0:1, 0:1]
        scale = lax.rsqrt(jnp.sum(q, axis=1, keepdims=True) * (1.0 / BINS) * (u * u) + 1e-05) * u
        for n in range(NCH):
            bbuf[slot * 256:slot * 256 + ROWS, n * CH:(n + 1) * CH] = (
                fr[:, n * CH:(n + 1) * CH] * scale).astype(bf16)

    lag = lag_ref[0]

    def to_columns(src, slot):
        mean = jnp.transpose(jnp.dot(raw[src], wsum[...], preferred_element_type=f32) * (1.0 / BINS))[0:8]
        q = jnp.zeros((4, 8, 128), f32)
        for n in range(NCH):
            if n == 0:
                got = lax.dot_general(wcol[:, PAD:WIN], raw[src, :, 0:CH], (((1,), (1,)), ((), ())),
                                      preferred_element_type=f32)
            else:
                got = lax.dot_general(wcol[...], raw[src, :, n * CH - PAD:(n + 1) * CH], (((1,), (1,)), ((), ())),
                                      preferred_element_type=f32)
            r = got.reshape(32, 8, 128) - mean[None] - popt[n * CH:(n + 1) * CH, :].reshape(32, 8, 128)
            ft[n * CH:(n + 1) * CH, :] = r.reshape(CH, 128)
            r = r * r
            for j in range(8):
                q = q + r[4 * j:4 * j + 4]
        q = (q[0] + q[1]) + (q[2] + q[3])
        u = unit[0:1]
        scale = lax.rsqrt(jnp.sum(q, axis=0, keepdims=True) * (1.0 / BINS) * (u * u) + 1e-05) * u * (1.0 / BINS)
        for n in range(NCH):
            wz[slot, n * CH:(n + 1) * CH, :] = (ft[n * CH:(n + 1) * CH, :] * scale).astype(bf16)
            ws[slot, n * CH:(n + 1) * CH, :] = (ft[pl.ds(n * CH + lag, CH), :] * scale).astype(bf16)

    def move(slot):
        for n in range(NCH):
            ft[n * CH:(n + 1) * CH, :] = wz[slot, n * CH:(n + 1) * CH, :].astype(f32)
        for n in range(NCH):
            ws[slot, n * CH:(n + 1) * CH, :] = ft[pl.ds(n * CH + lag, CH), :].astype(bf16)

    def place(s, major, minor):
        j, i = s // 2, s % 2
        z = (major + i * ((j + 1) % 2) + j // 3) % 2
        return z * 4 + (minor + (j % 2) * (3 + 2 * i) + (j // 2) * (1 - j % 2) * 2) % 4

    def whole(s, pairs=1):
        return [(s * 256 + k * ROWS, ROWS, (place(s + k // 2, zl, y) * 2 + (c if k % 2 == 0 else 1 - c)) * ROWS)
                for k in range(2 * pairs)]

    def halves(s, h):
        return [(s * 256 + k * ROWS + h * HALF, HALF, (place(s, zl, y) * 2 + (c if k == 0 else 1 - c)) * ROWS + h * HALF)
                for k in range(2)]

    def multiply(segments, groups):
        runs = []
        for first, size, _ in segments:
            if runs and isinstance(first, int) and runs[-1][0] + runs[-1][1] == first:
                runs[-1][1] += size
            else:
                runs.append([first, size])
        left = [bbuf[first:first + size, :] if isinstance(first, int) else bbuf[pl.ds(first, size), :]
                for first, size in runs]
        left = left[0] if len(left) == 1 else jnp.concatenate(left, axis=0)
        for g in groups:
            right = jnp.concatenate([ws[g], wz[g, LAGMAX:LAGMAX + BINS, :]], axis=1)
            out = jnp.dot(left, right, preferred_element_type=f32)
            gg, k = place(g, zh, x), 0
            for _, size, there in segments:
                there = pl.ds(pl.multiple_of(there, size), size)
                acc_ref[0, gg, there, :] = out[k:k + size, 0:128].astype(bf16)
                acc_ref[1, gg, there, :] = out[k:k + size, 128:256].astype(bf16)
                k += size

    def multiply_pairs(first, count, pairs, groups):
        def one(n, _):
            s = first + n * pairs
            start_row = pl.multiple_of(s * 256, 256)
            left = bbuf[pl.ds(start_row, pairs * 256), :]
            for g in groups:
                right = jnp.concatenate([ws[g], wz[g, LAGMAX:LAGMAX + BINS, :]], axis=1)
                out = jnp.dot(left, right, preferred_element_type=f32)
                gg = place(g, zh, x)
                for k, (_, size, there) in enumerate(whole(s, pairs)):
                    there = pl.ds(pl.multiple_of(there, size), size)
                    acc_ref[0, gg, there, :] = out[k * size:(k + 1) * size, 0:128].astype(bf16)
                    acc_ref[1, gg, there, :] = out[k * size:(k + 1) * size, 128:256].astype(bf16)
            return 0
        lax.fori_loop(0, count, one, 0)

    near = (S_O, S_Z, S_M, S_P)
    to_rows(O, S_O)
    start(("c", S_O))
    arrived(("zq", 3))
    start(("zo", 3))
    to_rows(QZ, S_Z)
    start(("qyp", 0), ("qym", 1), ("qyp", 1), ("qym", 0), ("c", S_Z))
    to_columns(O, S_O)
    arrived(("xp", 1), ("xm", 0), ("yp", 1), ("ym", 0))
    to_columns(XM, S_M)
    to_columns(XP, S_P)
    to_rows(YM, S_M)
    start(("c", S_M))
    arrived(("zo", 0), ("zo", 1), ("zo", 2), ("zo", 3))
    to_columns(PZ, S_Z)
    start(("pxp", 0), ("pxm", 1), ("pxp", 1), ("pxm", 0))
    to_rows(YP, S_P)
    start(("c", S_P))
    arrived("y2p", "y2m")
    to_rows(Y2, S_2)
    start(("zy", 0), ("zy", 1), ("c", S_2))
    arrived(("c", S_O), ("c", S_Z))
    multiply_pairs(S_O, 2, 1, near)
    arrived("x2p", "x2m")
    to_columns(X2, S_2)
    arrived(("c", S_M), ("c", S_P), ("c", S_2))
    multiply_pairs(S_M, 3, 1, near)
    arrived(("qyp", 0), ("qym", 1))
    start(("c", S_ZM, 0), ("c", S_ZP, 1))
    arrived(("pxp", 0), ("pxm", 1))
    start("px2p", "px2m")
    multiply(whole(S_O, 5), (S_2,))
    early = halves(S_ZM, 0) + halves(S_ZP, 1)
    later = halves(S_ZM, 1) + halves(S_ZP, 0)
    arrived(("c", S_ZM, 0), ("c", S_ZP, 1))
    multiply(early, near + (S_2,))
    arrived(("qyp", 1), ("qym", 0))
    start(("c", S_ZM, 1), ("c", S_ZP, 0))
    arrived(("pxp", 1), ("pxm", 0))
    move(S_ZM)
    move(S_ZP)
    multiply_pairs(S_O, 2, 2, (S_ZM, S_ZP))
    multiply(whole(S_2) + early, (S_ZM, S_ZP))
    arrived(("zy", 0), ("zy", 1))
    start(("c", S_Z2, 0), ("c", S_Z2, 1))
    arrived(("c", S_ZM, 1), ("c", S_ZP, 0))
    multiply(later, near + (S_2, S_ZM, S_ZP))
    arrived(("c", S_Z2, 0), ("c", S_Z2, 1))
    multiply(whole(S_Z2), near + (S_2, S_ZM, S_ZP))
    arrived("px2p", "px2m")
    move(S_Z2)
    multiply_pairs(S_O, 2, 4, (S_Z2,))

    for s in step1 + step2:
        s.wait_send()
    for name in copies:
        copies[name].wait_send()


N_COPIES = 2 * 12 + 8 + 6 + 5


def gathered(taps, lags, counts):
    dma = pltpu.SemaphoreType.DMA
    return pl.pallas_call(
        gather_kernel,
        out_shape=jax.ShapeDtypeStruct((2, 8, 2048, 128), bf16),
        in_specs=[pl.BlockSpec(memory_space=pltpu.HBM)] * 3,
        out_specs=pl.BlockSpec(memory_space=pltpu.VMEM),
        scratch_shapes=[
            pltpu.SMEM((TAPS,), jnp.int32),
            pltpu.SMEM((2,), jnp.int32),
            pltpu.VMEM((ROWS, BINS), jnp.int32),
            pltpu.VMEM((9, ROWS, BINS), bf16),
            pltpu.VMEM((2048, BINS), bf16),
            pltpu.VMEM((8, BINS + LAGMAX, 128), bf16),
            pltpu.VMEM((8, BINS, 128), bf16),
            pltpu.VMEM((BINS + LAGMAX, 128), f32),
            pltpu.VMEM((ROWS, BINS), f32),
            pltpu.VMEM((BINS, 128), f32),
            pltpu.VMEM((8, BINS), f32),
            pltpu.VMEM((WIN, CH), bf16),
            pltpu.VMEM((CH, WIN), bf16),
            pltpu.VMEM((BINS, 128), bf16),
            pltpu.VMEM((1, BINS), f32),
            pltpu.VMEM((1, BINS), f32),
            pltpu.VMEM((7, 1, BINS), f32),
            pltpu.VMEM((15, 1, BINS), f32),
            dma((4,)), dma((7,)), dma((7,)), dma((15,)), dma((15,)),
            dma((N_COPIES,)), dma((N_COPIES,)),
        ],
        compiler_params=pltpu.CompilerParams(
            collective_id=0, has_side_effects=True, vmem_limit_bytes=44 << 20),
        name="gather_products",
    )(*(pltpu.with_memory_space_constraint(a, pltpu.HBM) for a in (taps, lags, counts)))


def layout_kernel(acc_ref, out_ref, buf, sem):
    rows, slots = buf.shape[1], buf.shape[0]
    steps = 2048 // rows
    puts = []
    for s in range(2 * steps):
        lag, first = s // steps, (s % steps) * rows
        if s >= slots:
            puts[s - slots].wait()
        buf[s % slots] = jnp.swapaxes(acc_ref[lag, :, first:first + rows, :], 0, 1)
        put = pltpu.make_async_copy(buf.at[s % slots], out_ref.at[lag, first:first + rows], sem.at[s % slots])
        put.start()
        puts.append(put)
    for put in puts[-slots:]:
        put.wait()


def laid_out(acc):
    rows, slots = 256, 8
    return pl.pallas_call(
        layout_kernel,
        out_shape=jax.ShapeDtypeStruct((2, 2048, 8, 128), bf16),
        in_specs=[pl.BlockSpec(memory_space=pltpu.VMEM)],
        out_specs=pl.BlockSpec(memory_space=pl.ANY),
        scratch_shapes=[pltpu.VMEM((slots, rows, 8, 128), bf16), pltpu.SemaphoreType.DMA((slots,))],
        compiler_params=pltpu.CompilerParams(vmem_limit_bytes=24 << 20),
        name="layout",
    )(acc)


def shards(spike_counts, kernel_taps, lag_bins):
    return laid_out(gathered(kernel_taps, lag_bins, spike_counts))


def solution(mesh):
    placed = (P(("row", "blk"), None), P(), P())
    return jax.shard_map(
        shards, mesh=mesh, in_specs=placed, out_specs=P(None, "row", None, "blk"), check_vma=False
    )
```

```python
import functools

import jax
import jax.numpy as jnp
from jax import lax
from jax.experimental import pallas as pl
from jax.experimental.pallas import tpu as pltpu
from jax.sharding import PartitionSpec as P

NEURONS = 16384
BINS = 2048
TAPS = 16
LAGMAX = 32
MESH = pl.DeviceIdType.MESH
f32 = jnp.float32
bf16 = jnp.bfloat16

ROWS = 128
HALF = ROWS // 2
PAD = 128
CH = 256
NCH = BINS // CH
WIN = CH + PAD
QUARTER = ROWS // 4

O, XM, XP, X2, PZ, YM, YP, Y2, QZ = range(9)
S_O, S_Z, S_M, S_P, S_2, S_Z2, S_ZM, S_ZP = range(8)


def gather_kernel(taps_hbm, lag_hbm, counts_hbm, acc_ref,
                  taps_ref, lag_ref, counts, raw, bbuf, wz, ws, ft, fr, popt, popr, wrow, wcol, wsum,
                  own_sum, part_sum, got1, got2, lsem, snd1, rcv1, snd2, rcv2, ssem, rsem):
    row = lax.axis_index("row")
    blk = lax.axis_index("blk")
    zh, x = row // 4, row % 4
    zl, y, c = blk // 8, (blk // 2) % 4, blk % 2

    loads = [pltpu.make_async_copy(counts_hbm.at[h * HALF:(h + 1) * HALF, :],
                                   counts.at[h * HALF:(h + 1) * HALF, :], lsem.at[h]) for h in range(2)]
    loads += [pltpu.make_async_copy(taps_hbm, taps_ref, lsem.at[2]),
              pltpu.make_async_copy(lag_hbm, lag_ref, lsem.at[3])]
    for load in loads:
        load.start()

    def at(zh_, x_, zl_, y_, c_):
        return {"row": zh_ * 4 + x_, "blk": zl_ * 8 + y_ * 2 + c_}

    xp = at(zh, (x + 1) % 4, zl, y, c)
    xm = at(zh, (x + 3) % 4, zl, y, c)
    yp = at(zh, x, zl, (y + 1) % 4, c)
    ym = at(zh, x, zl, (y + 3) % 4, c)
    zq = at(zh, x, 1 - zl, y, c)
    zo = at(1 - zh, x, 1 - zl, y, c)
    cp = at(zh, x, zl, y, 1 - c)

    barrier = pltpu.get_barrier_semaphore()
    for d in range(1, 8):
        pl.semaphore_signal(barrier, inc=1, device_id={"row": (row + d) % 8, "blk": blk}, device_id_type=MESH)
    for d in range(1, 16):
        pl.semaphore_signal(barrier, inc=1, device_id={"row": row, "blk": (blk + d) % 16}, device_id_type=MESH)
    pl.semaphore_signal(barrier, inc=1, device_id=zo, device_id_type=MESH)

    for h in range(2):
        loads[h].wait()
        for n in range(NCH):
            part = counts[h * HALF:(h + 1) * HALF, n * CH:(n + 1) * CH].astype(f32)
            raw[O, h * HALF:(h + 1) * HALF, n * CH:(n + 1) * CH] = part.astype(bf16)
            part = jnp.sum(part, axis=0, keepdims=True)
            own_sum[:, n * CH:(n + 1) * CH] = part if h == 0 else own_sum[:, n * CH:(n + 1) * CH] + part
    pl.semaphore_wait(barrier, 23)

    step1 = [pltpu.make_async_remote_copy(
        src_ref=own_sum, dst_ref=got1.at[d - 1], send_sem=snd1.at[d - 1], recv_sem=rcv1.at[d - 1],
        device_id={"row": (row + d) % 8, "blk": blk}, device_id_type=MESH) for d in range(1, 8)]
    step2 = [pltpu.make_async_remote_copy(
        src_ref=part_sum, dst_ref=got2.at[d - 1], send_sem=snd2.at[d - 1], recv_sem=rcv2.at[d - 1],
        device_id={"row": row, "blk": (blk + d) % 16}, device_id_type=MESH) for d in range(1, 16)]

    copies = {}

    def copy(name, src, dst, device):
        k = len(copies)
        copies[name] = pltpu.make_async_remote_copy(
            src_ref=src, dst_ref=dst, send_sem=ssem.at[k], recv_sem=rsem.at[k],
            device_id=device, device_id_type=MESH)

    def start(*names):
        for name in names:
            copies[name].start()

    def arrived(*names):
        for name in names:
            copies[name].wait_recv()

    def raw_half(slot, h):
        return raw.at[slot, h * HALF:(h + 1) * HALF, :]

    def raw_quarter(slot, k):
        return raw.at[slot, k * QUARTER:(k + 1) * QUARTER, :]

    def wz_half(slot, h):
        return wz.at[slot, h * (BINS // 2):(h + 1) * (BINS // 2), :]

    def bb_half(slot, h, other=0):
        first = slot * 256 + other * ROWS + h * HALF
        return bbuf.at[first:first + HALF, :]

    for h in range(2):
        copy(("xp", h), raw_half(O, h), raw_half(XM, h), xp)
        copy(("xm", h), raw_half(O, h), raw_half(XP, h), xm)
        copy(("yp", h), raw_half(O, h), raw_half(YM, h), yp)
        copy(("ym", h), raw_half(O, h), raw_half(YP, h), ym)
        copy(("pxp", h), wz_half(S_Z, h), wz_half(S_ZM, h), xp)
        copy(("pxm", h), wz_half(S_Z, h), wz_half(S_ZP, h), xm)
        copy(("qyp", h), bb_half(S_Z, h), bb_half(S_ZM, h), yp)
        copy(("qym", h), bb_half(S_Z, h), bb_half(S_ZP, h), ym)
        copy(("zy", h), bb_half(S_2, h), bb_half(S_Z2, h), zq)
        for slot in (S_Z2, S_ZM, S_ZP):
            copy(("c", slot, h), bb_half(slot, h), bb_half(slot, h, 1), cp)
    for k in range(4):
        copy(("zq", k), raw_quarter(O, k), raw_quarter(QZ, k), zq)
        copy(("zo", k), raw_quarter(QZ, k), raw_quarter(PZ, k), zo)
    copy("x2p", raw_half(XM, 0), raw_half(X2, 0), xp)
    copy("x2m", raw_half(XP, 1), raw_half(X2, 1), xm)
    copy("y2p", raw_half(YM, 0), raw_half(Y2, 0), yp)
    copy("y2m", raw_half(YP, 1), raw_half(Y2, 1), ym)
    copy("px2p", wz_half(S_ZM, 0), wz_half(S_Z2, 0), xp)
    copy("px2m", wz_half(S_ZP, 1), wz_half(S_Z2, 1), xm)
    for slot in (S_O, S_Z, S_M, S_P, S_2):
        copy(("c", slot), bbuf.at[slot * 256:slot * 256 + ROWS, :],
             bbuf.at[slot * 256 + ROWS:slot * 256 + 2 * ROWS, :], cp)

    for s in step1:
        s.start()
    start(("zq", 0), ("xp", 0), ("xm", 1), ("yp", 0), ("ym", 1), ("zq", 1))

    loads[2].wait()
    loads[3].wait()
    taps = [taps_ref[k].astype(f32) for k in range(TAPS)]
    total = sum(taps[1:], taps[0])
    unit = 1.0 / jnp.full((8, 128), total, f32)
    late = lax.broadcasted_iota(jnp.int32, (WIN, CH), 1) + PAD - lax.broadcasted_iota(jnp.int32, (WIN, CH), 0)
    band = jnp.zeros((WIN, CH), f32)
    for k in range(TAPS):
        band = jnp.where(late == k, taps[k], band)
    wrow[...] = band.astype(bf16)
    late = lax.broadcasted_iota(jnp.int32, (CH, WIN), 0) + PAD - lax.broadcasted_iota(jnp.int32, (CH, WIN), 1)
    band = jnp.zeros((CH, WIN), f32)
    for k in range(TAPS):
        band = jnp.where(late == k, taps[k], band)
    wcol[...] = band.astype(bf16)
    wsum[...] = jnp.full((BINS, 128), total, f32).astype(bf16)
    left = TAPS - lax.broadcasted_iota(jnp.int32, (TAPS, 128), 0)
    edge = jnp.zeros((TAPS, 128), f32)
    for k in range(TAPS):
        edge = edge + jnp.where(left > k, taps[k], 0.0)
    wsum[BINS - TAPS:BINS, :] = edge.astype(bf16)
    ft[BINS:BINS + LAGMAX, :] = jnp.zeros((LAGMAX, 128), f32)
    for k in range(8):
        wz[k, BINS:BINS + LAGMAX, :] = jnp.zeros((LAGMAX, 128), bf16)

    for s in step1:
        s.wait_recv()
    part_sum[...] = own_sum[...] + sum([got1[d] for d in range(1, 7)], got1[0])
    for s in step2:
        s.start()
    start(("zq", 2), ("xp", 1), ("xm", 0), ("yp", 1), ("ym", 0), ("zq", 3))
    arrived(("zq", 0))
    start(("zo", 0))
    arrived(("xp", 0), ("xm", 1))
    start("x2p", "x2m")
    arrived(("yp", 0), ("ym", 1))
    start("y2p", "y2m")
    arrived(("zq", 1))
    start(("zo", 1))
    arrived(("zq", 2))
    start(("zo", 2))

    for s in step2:
        s.wait_recv()
    alls = part_sum[...] + sum([got2[d] for d in range(1, 15)], got2[0])
    high = alls.astype(bf16)
    rest = alls - high.astype(f32)
    mid = rest.astype(bf16)
    low = (rest - mid.astype(f32)).astype(bf16)
    summed = jnp.zeros((8, 128), f32)
    for n in range(NCH):
        first = max(n * CH - PAD, 0)
        wins = jnp.concatenate(
            [jnp.broadcast_to(piece[:, first:(n + 1) * CH], (16, (n + 1) * CH - first)) for piece in (high, mid, low)],
            axis=0)
        got = jnp.dot(wins, wrow[PAD:WIN, :] if n == 0 else wrow[...], preferred_element_type=f32)
        got = (got[0:8] + got[16:24]) + got[32:40]
        popr[:, n * CH:(n + 1) * CH] = got
        summed = summed + (got[:, 0:128] + got[:, 128:256])
    mean_pop = jnp.sum(summed, axis=1, keepdims=True) * (1.0 / BINS)
    popr[...] = (popr[...] - mean_pop) * (1.0 / NEURONS)
    for n in range(BINS // 128):
        popt[n * 128:(n + 1) * 128, :] = jnp.transpose(
            jnp.broadcast_to(popr[0:1, n * 128:(n + 1) * 128], (128, 128)))

    def to_rows(src, slot):
        mean = jnp.dot(raw[src], wsum[...], preferred_element_type=f32) * (1.0 / BINS)
        mean = jnp.concatenate([mean, mean], axis=1)
        q = jnp.zeros((ROWS, 128), f32)
        for n in range(NCH):
            if n == 0:
                got = jnp.dot(raw[src, :, 0:CH], wrow[PAD:WIN, :], preferred_element_type=f32)
            else:
                got = jnp.dot(raw[src, :, n * CH - PAD:(n + 1) * CH], wrow[...], preferred_element_type=f32)
            r = got - mean - popr[0:1, n * CH:(n + 1) * CH]
            fr[:, n * CH:(n + 1) * CH] = r
            r = r * r
            q = q + r[:, 0:128] + r[:, 128:256]
        u = unit[0:1, 0:1]
        scale = lax.rsqrt(jnp.sum(q, axis=1, keepdims=True) * (1.0 / BINS) * (u * u) + 1e-05) * u
        for n in range(NCH):
            bbuf[slot * 256:slot * 256 + ROWS, n * CH:(n + 1) * CH] = (
                fr[:, n * CH:(n + 1) * CH] * scale).astype(bf16)

    lag = lag_ref[0]

    def to_columns(src, slot):
        mean = jnp.transpose(jnp.dot(raw[src], wsum[...], preferred_element_type=f32) * (1.0 / BINS))[0:8]
        q = jnp.zeros((4, 8, 128), f32)
        for n in range(NCH):
            if n == 0:
                got = lax.dot_general(wcol[:, PAD:WIN], raw[src, :, 0:CH], (((1,), (1,)), ((), ())),
                                      preferred_element_type=f32)
            else:
                got = lax.dot_general(wcol[...], raw[src, :, n * CH - PAD:(n + 1) * CH], (((1,), (1,)), ((), ())),
                                      preferred_element_type=f32)
            r = got.reshape(32, 8, 128) - mean[None] - popt[n * CH:(n + 1) * CH, :].reshape(32, 8, 128)
            ft[n * CH:(n + 1) * CH, :] = r.reshape(CH, 128)
            r = r * r
            for j in range(8):
                q = q + r[4 * j:4 * j + 4]
        q = (q[0] + q[1]) + (q[2] + q[3])
        u = unit[0:1]
        scale = lax.rsqrt(jnp.sum(q, axis=0, keepdims=True) * (1.0 / BINS) * (u * u) + 1e-05) * u * (1.0 / BINS)
        for n in range(NCH):
            wz[slot, n * CH:(n + 1) * CH, :] = (ft[n * CH:(n + 1) * CH, :] * scale).astype(bf16)
            ws[slot, n * CH:(n + 1) * CH, :] = (ft[pl.ds(n * CH + lag, CH), :] * scale).astype(bf16)

    def move(slot):
        for n in range(NCH):
            ft[n * CH:(n + 1) * CH, :] = wz[slot, n * CH:(n + 1) * CH, :].astype(f32)
        for n in range(NCH):
            ws[slot, n * CH:(n + 1) * CH, :] = ft[pl.ds(n * CH + lag, CH), :].astype(bf16)

    def place(s, major, minor):
        j, i = s // 2, s % 2
        z = (major + i * ((j + 1) % 2) + j // 3) % 2
        return z * 4 + (minor + (j % 2) * (3 + 2 * i) + (j // 2) * (1 - j % 2) * 2) % 4

    def whole(s, pairs=1):
        return [(s * 256 + k * ROWS, ROWS, (place(s + k // 2, zl, y) * 2 + (c if k % 2 == 0 else 1 - c)) * ROWS)
                for k in range(2 * pairs)]

    def halves(s, h):
        return [(s * 256 + k * ROWS + h * HALF, HALF, (place(s, zl, y) * 2 + (c if k == 0 else 1 - c)) * ROWS + h * HALF)
                for k in range(2)]

    def multiply(segments, groups):
        runs = []
        for first, size, _ in segments:
            if runs and isinstance(first, int) and runs[-1][0] + runs[-1][1] == first:
                runs[-1][1] += size
            else:
                runs.append([first, size])
        left = [bbuf[first:first + size, :] if isinstance(first, int) else bbuf[pl.ds(first, size), :]
                for first, size in runs]
        left = left[0] if len(left) == 1 else jnp.concatenate(left, axis=0)
        for g in groups:
            right = jnp.concatenate([ws[g], wz[g, LAGMAX:LAGMAX + BINS, :]], axis=1)
            out = jnp.dot(left, right, preferred_element_type=f32)
            gg, k = place(g, zh, x), 0
            for _, size, there in segments:
                there = pl.ds(pl.multiple_of(there, size), size)
                acc_ref[0, gg, there, :] = out[k:k + size, 0:128].astype(bf16)
                acc_ref[1, gg, there, :] = out[k:k + size, 128:256].astype(bf16)
                k += size

    def multiply_pairs(first, count, pairs, groups):
        def one(n, _):
            s = first + n * pairs
            start_row = pl.multiple_of(s * 256, 256)
            left = bbuf[pl.ds(start_row, pairs * 256), :]
            for g in groups:
                right = jnp.concatenate([ws[g], wz[g, LAGMAX:LAGMAX + BINS, :]], axis=1)
                out = jnp.dot(left, right, preferred_element_type=f32)
                gg = place(g, zh, x)
                for k, (_, size, there) in enumerate(whole(s, pairs)):
                    there = pl.ds(pl.multiple_of(there, size), size)
                    acc_ref[0, gg, there, :] = out[k * size:(k + 1) * size, 0:128].astype(bf16)
                    acc_ref[1, gg, there, :] = out[k * size:(k + 1) * size, 128:256].astype(bf16)
            return 0
        lax.fori_loop(0, count, one, 0)

    near = (S_O, S_Z, S_M, S_P)
    to_rows(O, S_O)
    start(("c", S_O))
    arrived(("zq", 3))
    start(("zo", 3))
    to_rows(QZ, S_Z)
    start(("qyp", 0), ("qym", 1), ("qyp", 1), ("qym", 0), ("c", S_Z))
    to_columns(O, S_O)
    arrived(("xp", 1), ("xm", 0), ("yp", 1), ("ym", 0))
    to_columns(XM, S_M)
    to_columns(XP, S_P)
    to_rows(YM, S_M)
    start(("c", S_M))
    arrived(("zo", 0), ("zo", 1), ("zo", 2), ("zo", 3))
    to_columns(PZ, S_Z)
    start(("pxp", 0), ("pxm", 1), ("pxp", 1), ("pxm", 0))
    to_rows(YP, S_P)
    start(("c", S_P))
    arrived("y2p", "y2m")
    to_rows(Y2, S_2)
    start(("zy", 0), ("zy", 1), ("c", S_2))
    arrived(("c", S_O), ("c", S_Z))
    multiply_pairs(S_O, 2, 1, near)
    arrived("x2p", "x2m")
    to_columns(X2, S_2)
    arrived(("c", S_M), ("c", S_P), ("c", S_2))
    multiply_pairs(S_M, 3, 1, near)
    arrived(("qyp", 0), ("qym", 1))
    start(("c", S_ZM, 0), ("c", S_ZP, 1))
    arrived(("pxp", 0), ("pxm", 1))
    start("px2p", "px2m")
    multiply(whole(S_O, 5), (S_2,))
    early = halves(S_ZM, 0) + halves(S_ZP, 1)
    later = halves(S_ZM, 1) + halves(S_ZP, 0)
    arrived(("c", S_ZM, 0), ("c", S_ZP, 1))
    multiply(early, near + (S_2,))
    arrived(("qyp", 1), ("qym", 0))
    start(("c", S_ZM, 1), ("c", S_ZP, 0))
    arrived(("pxp", 1), ("pxm", 0))
    move(S_ZM)
    move(S_ZP)
    multiply_pairs(S_O, 2, 2, (S_ZM, S_ZP))
    multiply(whole(S_2) + early, (S_ZM, S_ZP))
    arrived(("zy", 0), ("zy", 1))
    start(("c", S_Z2, 0), ("c", S_Z2, 1))
    arrived(("c", S_ZM, 1), ("c", S_ZP, 0))
    multiply(later, near + (S_2, S_ZM, S_ZP))
    arrived(("c", S_Z2, 0), ("c", S_Z2, 1))
    multiply(whole(S_Z2), near + (S_2, S_ZM, S_ZP))
    arrived("px2p", "px2m")
    move(S_Z2)
    multiply(whole(S_O, 8), (S_Z2,))

    for s in step1 + step2:
        s.wait_send()
    for name in copies:
        copies[name].wait_send()


N_COPIES = 2 * 12 + 8 + 6 + 5


def gathered(taps, lags, counts):
    dma = pltpu.SemaphoreType.DMA
    return pl.pallas_call(
        gather_kernel,
        out_shape=jax.ShapeDtypeStruct((2, 8, 2048, 128), bf16),
        in_specs=[pl.BlockSpec(memory_space=pltpu.HBM)] * 3,
        out_specs=pl.BlockSpec(memory_space=pltpu.VMEM),
        scratch_shapes=[
            pltpu.SMEM((TAPS,), jnp.int32),
            pltpu.SMEM((2,), jnp.int32),
            pltpu.VMEM((ROWS, BINS), jnp.int32),
            pltpu.VMEM((9, ROWS, BINS), bf16),
            pltpu.VMEM((2048, BINS), bf16),
            pltpu.VMEM((8, BINS + LAGMAX, 128), bf16),
            pltpu.VMEM((8, BINS, 128), bf16),
            pltpu.VMEM((BINS + LAGMAX, 128), f32),
            pltpu.VMEM((ROWS, BINS), f32),
            pltpu.VMEM((BINS, 128), f32),
            pltpu.VMEM((8, BINS), f32),
            pltpu.VMEM((WIN, CH), bf16),
            pltpu.VMEM((CH, WIN), bf16),
            pltpu.VMEM((BINS, 128), bf16),
            pltpu.VMEM((1, BINS), f32),
            pltpu.VMEM((1, BINS), f32),
            pltpu.VMEM((7, 1, BINS), f32),
            pltpu.VMEM((15, 1, BINS), f32),
            dma((4,)), dma((7,)), dma((7,)), dma((15,)), dma((15,)),
            dma((N_COPIES,)), dma((N_COPIES,)),
        ],
        compiler_params=pltpu.CompilerParams(
            collective_id=0, has_side_effects=True, vmem_limit_bytes=44 << 20),
        name="gather_products",
    )(*(pltpu.with_memory_space_constraint(a, pltpu.HBM) for a in (taps, lags, counts)))


def layout_kernel(acc_ref, out_ref, buf, sem):
    rows, slots = buf.shape[1], buf.shape[0]
    steps = 2048 // rows
    puts = []
    for s in range(2 * steps):
        lag, first = s // steps, (s % steps) * rows
        if s >= slots:
            puts[s - slots].wait()
        buf[s % slots] = jnp.swapaxes(acc_ref[lag, :, first:first + rows, :], 0, 1)
        put = pltpu.make_async_copy(buf.at[s % slots], out_ref.at[lag, first:first + rows], sem.at[s % slots])
        put.start()
        puts.append(put)
    for put in puts[-slots:]:
        put.wait()


def laid_out(acc):
    rows, slots = 256, 8
    return pl.pallas_call(
        layout_kernel,
        out_shape=jax.ShapeDtypeStruct((2, 2048, 8, 128), bf16),
        in_specs=[pl.BlockSpec(memory_space=pltpu.VMEM)],
        out_specs=pl.BlockSpec(memory_space=pl.ANY),
        scratch_shapes=[pltpu.VMEM((slots, rows, 8, 128), bf16), pltpu.SemaphoreType.DMA((slots,))],
        compiler_params=pltpu.CompilerParams(vmem_limit_bytes=24 << 20),
        name="layout",
    )(acc)


def shards(spike_counts, kernel_taps, lag_bins):
    return laid_out(gathered(kernel_taps, lag_bins, spike_counts))


def solution(mesh):
    placed = (P(("row", "blk"), None), P(), P())
    return jax.shard_map(
        shards, mesh=mesh, in_specs=placed, out_specs=P(None, "row", None, "blk"), check_vma=False
    )
```
